128 devices in a mesh: row: 16 (over x, z), col: 8 (over y, core).
Axes of the slice: x: 4, y: 4, z: 4, core: 2. Of those that a mesh axis runs over, the one named last changes fastest.
Arguments:
- raw_weight: float32 [6144, 6144], P('row', 'col'), may hold values from -0.2 to 1.2
- features: bfloat16 [2048, 6144], P(None, 'row'), may hold values from -6 to 6
- head: bfloat16 [100, 6144], P(None, 'col'), may hold values from -0.078125 to 0.078125
- labels: int32 [2048], P('row'), may hold values from 0 to 99
Outputs:
- ortho_weight: float32 [6144, 6144], P('row', 'col')
- row_loss: float32 [2048], P('row')
- weight_grad: float32 [6144, 6144], P('row', 'col')
- head_grad: float32 [100, 6144], P(None, 'col')
The draws below stay inside these ranges and needn't reach their ends.
All inputs are finite; a program needn't handle non-finite values.
Results may differ from the reference program's by a relative error of at most 0.018.
Values may be sent and summed in bfloat16 or wider, within the bound.
A program may use at most 64 MiB of HBM per device.

```python
import math
import jax
import jax.numpy as jnp
from jax import lax

D = 6144
CLASSES = 100
ITERS = 2
TOKENS = 2048
N_ROW = 16
N_COL = 8


def draw_raw_weight(key, part):
    first_key = jax.random.fold_in(key, 0)
    diagonal = (lax.broadcasted_iota(jnp.int32, (D, D), 0) == lax.broadcasted_iota(jnp.int32, (D, D), 1)).astype(jnp.float32)
    noise = jnp.clip(jax.random.normal(first_key, (D, D), jnp.float32), -4.0, 4.0)
    return diagonal + 0.35 * noise / math.sqrt(D)


def touch_ends(drawn, key, low, high):
    dims = drawn.shape
    index_at = [jax.random.randint(jax.random.fold_in(key, axis), (), 0, dims[axis]) for axis in range(len(dims))]
    drawn = drawn.at[tuple(index_at)].set(low)
    longest = dims.index(max(dims))
    index_at[longest] = (index_at[longest] + 1) % dims[longest]
    return drawn.at[tuple(index_at)].set(high)


def strengthened(values, stream_key, source, target, shards_of, factor):
    def block_of(axis_at):
        return (jnp.arange(values.shape[axis_at]) // (values.shape[axis_at] // shards_of)).reshape((-1,) + (1,) * (values.ndim - 1 - axis_at))

    near = jax.random.permutation(stream_key, shards_of)[block_of(target)]
    other_side = (block_of(target) + shards_of // 2) % shards_of
    return jnp.where((block_of(source) == near) | (block_of(source) == other_side), factor * values, values)


def levels(rng, shape, shards, low, high):
    def one(axis_at, parts):
        steps = jax.random.uniform(jax.random.fold_in(jax.random.fold_in(rng, 6), axis_at), (parts,), jnp.float32, low / len(shards), high / len(shards))
        return jnp.repeat(jnp.exp(steps), shape[axis_at] // parts).reshape((-1,) + (1,) * (len(shape) - axis_at - 1))

    factor_of = one(*shards[0])
    for cut in shards[1:]:
        factor_of = factor_of * one(*cut)
    return factor_of


def normal_values(own_key, extent, scale, reach, shards=(), held_as=jnp.bfloat16):
    entries = scale * jax.random.normal(own_key, extent, jnp.float32)
    if shards:
        entries = entries * levels(own_key, extent, shards, -0.22, 0.18)
    return jnp.clip(entries, -reach, reach).astype(held_as)


def gaussian_with(key, extent, spread, most, cuts, heavy, kind=jnp.bfloat16):
    entries = spread * jax.random.normal(key, extent, jnp.float32)
    if cuts:
        entries = entries * levels(key, extent, cuts, -0.22, 0.18)
    return jnp.clip(strengthened(entries, jax.random.fold_in(key, 3), *heavy), -most, most).astype(kind)


def setup_inputs(seed: int = 0) -> dict:
    keys = jax.random.split(jax.random.key(seed), 5)
    return {
        "raw_weight": draw_raw_weight(jax.random.fold_in(keys[4], 71), 0),
        "features": gaussian_with(keys[1], (TOKENS, D), 1.0, 6.0, ((1, 16),), (1, 0, 16, 2.0)),
        "head": normal_values(keys[2], (CLASSES, D), D ** -0.5, 0.078125, ((1, 8),)),
        "labels": touch_ends(jax.random.randint(keys[3], (TOKENS,), 0, CLASSES), jax.random.fold_in(keys[3], 1), 0, CLASSES - 1).astype(jnp.int32),
    }


def reference(raw_weight, features, head, labels):
    current = raw_weight
    col_width = D // N_COL
    pair = (((1,), (1,)), ((), ()))
    for iteration in range(ITERS):
        rounded = current.astype(jnp.bfloat16)
        gram = jnp.zeros((D, D), jnp.float32)
        for block_index in range(N_COL):
            block = rounded[:, block_index * col_width:(block_index + 1) * col_width]
            term = lax.dot_general(block, block, pair, preferred_element_type=jnp.float32)
            gram = gram + lax.optimization_barrier(term.astype(jnp.bfloat16)).astype(jnp.float32)
        product = jnp.dot(gram.astype(jnp.bfloat16), rounded, preferred_element_type=jnp.float32)
        current = 1.5 * current - 0.5 * product
    weight_bf = current.astype(jnp.bfloat16)
    row_width = D // N_ROW
    pre_sum = jnp.zeros((TOKENS, D), jnp.float32)
    for block_index in range(N_ROW):
        lower = block_index * row_width
        term = jnp.dot(features[:, lower:lower + row_width], weight_bf[lower:lower + row_width, :], preferred_element_type=jnp.float32)
        pre_sum = pre_sum + lax.optimization_barrier(term.astype(jnp.bfloat16)).astype(jnp.float32)
    activation = jnp.tanh(pre_sum)
    active_bf = activation.astype(jnp.bfloat16)
    class_ids = jnp.arange(CLASSES, dtype=jnp.int32)
    one_hot = (labels[:, None] == class_ids[None, :]).astype(jnp.float32)
    picked = jnp.dot(one_hot.astype(jnp.bfloat16), head, preferred_element_type=jnp.float32).astype(jnp.bfloat16)
    logits = lax.dot_general(active_bf, head, pair, preferred_element_type=jnp.float32)
    inner = lax.dot_general(picked, head, pair, preferred_element_type=jnp.float32)
    head_wide = head.astype(jnp.float32)
    norms_sq = lax.optimization_barrier(jnp.sum(head_wide * head_wide, axis=1))
    own_norm = lax.optimization_barrier(jnp.sum(one_hot * norms_sq[None, :], axis=1))
    distance = own_norm[:, None] + norms_sq[None, :] - 2.0 * inner + 1e-05
    lipschitz = jnp.sqrt(jnp.where(one_hot > 0, 1.0, distance))
    plain_exp = jnp.exp(logits)
    bound_exp = (1.0 - one_hot) * jnp.exp(logits + lipschitz)
    partition = lax.optimization_barrier(jnp.sum(plain_exp, axis=1)) + lax.optimization_barrier(jnp.sum(bound_exp, axis=1))
    row_loss = jnp.log(partition) - lax.optimization_barrier(jnp.sum(one_hot * logits, axis=1))
    logit_grad = (plain_exp + bound_exp) / partition[:, None] - one_hot
    dist_grad = bound_exp / (partition[:, None] * 2.0 * lipschitz)
    norm_grad = lax.optimization_barrier(jnp.sum(dist_grad, axis=0)) + lax.optimization_barrier(jnp.sum(one_hot * lax.optimization_barrier(jnp.sum(dist_grad, axis=1))[:, None], axis=0))
    highest = lax.Precision.HIGHEST
    head_grad = jnp.dot(logit_grad.T, active_bf.astype(jnp.float32), precision=highest) + 2.0 * norm_grad[:, None] * head_wide - 2.0 * jnp.dot(dist_grad.T, picked.astype(jnp.float32), precision=highest) - 2.0 * jnp.dot(one_hot.T, jnp.dot(dist_grad, head_wide, precision=highest), precision=highest)
    act_grad = jnp.dot(logit_grad, head_wide, precision=highest)
    pre_grad = (act_grad * (1.0 - activation * activation)).astype(jnp.bfloat16)
    weight_grad = jnp.dot(features.T, pre_grad, preferred_element_type=jnp.float32)
    return (current, row_loss, weight_grad, head_grad)
```

```python
import jax
import jax.numpy as jnp
from jax import lax
from jax.experimental import pallas as pl
from jax.experimental.pallas import tpu as pltpu
from jax.sharding import PartitionSpec as P

ITERS = 2
SIDE = 4
F32 = jnp.float32
BF16 = jnp.bfloat16
MESH = pl.DeviceIdType.MESH
NT = (((1,), (1,)), ((), ()))


class Copies:
    def __init__(self, send_sems, recv_sems):
        self.sems = (send_sems, recv_sems)
        self.started = {}

    def send(self, name, src, dst, device):
        index = len(self.started)
        copy = pltpu.make_async_remote_copy(
            src_ref=src, dst_ref=dst, send_sem=self.sems[0].at[index], recv_sem=self.sems[1].at[index],
            device_id=device, device_id_type=MESH,
        )
        copy.start()
        self.started[name] = copy

    def arrived(self, name):
        self.started[name].wait_recv()

    def drain(self):
        for copy in self.started.values():
            copy.wait_send()


def neighbours():
    row, col = lax.axis_index("row"), lax.axis_index("col")
    x, z, y, core = row // SIDE, row % SIDE, col // 2, col % 2
    up = lambda v, d: (v + d) % SIDE
    return dict(
        zp=(x * SIDE + up(z, 1), col), zm=(x * SIDE + up(z, 3), col),
        xp=(up(x, 1) * SIDE + z, col), xm=(up(x, 3) * SIDE + z, col),
        yp=(row, up(y, 1) * 2 + core), ym=(row, up(y, 3) * 2 + core),
        twin=(row, y * 2 + 1 - core),
    )


def greet(devices):
    barrier = pltpu.get_barrier_semaphore()
    for device in devices:
        pl.semaphore_signal(barrier, inc=1, device_id=device, device_id_type=MESH)
    pl.semaphore_wait(barrier, len(devices))


GROUPS = (2, 1, 3, 0)


def bjorck_kernel(w_ref, wb_ref, out_ref, outb_ref, az, ax, gp, gr, gh, gf, far, near, pb, pf, pq, send_sems, recv_sems):
    rows, cols = w_ref.shape
    half, quarter, wide = rows // 2, rows // 4, rows * SIDE
    col = lax.axis_index("col")
    y, core = col // 2, col % 2
    to = neighbours()
    greet(list(to.values()))
    net = Copies(send_sems, recv_sems)
    mine = pl.ds(pl.multiple_of(core * half, half), half)
    other = pl.ds(pl.multiple_of((1 - core) * half, half), half)

    def mine_part(part):
        return pl.ds(pl.multiple_of(core * half + part * quarter, quarter), quarter)

    def block(dy):
        return pl.ds(pl.multiple_of(((y + dy) % SIDE) * rows, rows), rows)

    lo, hi = pl.ds(0, half), pl.ds(half, half)
    axrow = lambda d, part: pl.ds(d * rows + part * half, half)
    net.send("zm0", wb_ref.at[lo], az.at[1, lo], to["zm"])
    net.send("xm0", wb_ref.at[lo], ax.at[axrow(1, 0)], to["xm"])
    net.send("zp0", wb_ref.at[hi], az.at[3, hi], to["zp"])
    net.send("xp0", wb_ref.at[hi], ax.at[axrow(3, 1)], to["xp"])
    net.send("zm1", wb_ref.at[hi], az.at[1, hi], to["zm"])
    net.send("xm1", wb_ref.at[hi], ax.at[axrow(1, 1)], to["xm"])
    net.send("zp1", wb_ref.at[lo], az.at[3, lo], to["zp"])
    net.send("xp1", wb_ref.at[lo], ax.at[axrow(3, 0)], to["xp"])
    az[0] = wb_ref[...]
    ax[0:rows, :] = wb_ref[...]
    net.arrived("zm0")
    net.send("zm2", az.at[1, lo], az.at[2, lo], to["zm"])
    net.arrived("xm0")
    net.send("xm2", ax.at[axrow(1, 0)], ax.at[axrow(2, 0)], to["xm"])
    net.arrived("zp0")
    net.send("zp2", az.at[3, hi], az.at[2, hi], to["zp"])
    net.arrived("xp0")
    net.send("xp2", ax.at[axrow(3, 1)], ax.at[axrow(2, 1)], to["xp"])
    for name in ("zm1", "xm1", "zp1", "xp1", "zm2", "xm2", "zp2", "xp2"):
        net.arrived(name)

    def partial_gram(g):
        @pl.loop(0, wide // 512)
        def _(n):
            at = pl.ds(pl.multiple_of(n * 512, 512), 512)
            gp[g, :, at] = lax.dot_general(az[g], ax[at, :], NT, preferred_element_type=F32).astype(BF16)
        net.send(("twin", g), gp.at[g, other], gr.at[g], to["twin"])

    def chip_sum(g):
        net.arrived(("twin", g))
        gh[g] = (gp[g, mine].astype(F32) + gr[g].astype(F32)).astype(BF16)
        net.send(("farp", g), gh.at[g, 0:quarter, block(2)], far.at[g, 0], to["yp"])
        net.send(("farm", g), gh.at[g, quarter:half, block(2)], far.at[g, 1], to["ym"])

    def far_sum(g):
        net.arrived(("farp", g))
        one = gh.at[g, 0:quarter, block(1)]
        one[...] = (one[...].astype(F32) + far[g, 0].astype(F32)).astype(BF16)
        net.send(("nearp", g), gh.at[g, :, block(1)], near.at[g, 0], to["yp"])
        net.arrived(("farm", g))
        two = gh.at[g, quarter:half, block(3)]
        two[...] = (two[...].astype(F32) + far[g, 1].astype(F32)).astype(BF16)
        net.send(("nearm", g), gh.at[g, :, block(3)], near.at[g, 1], to["ym"])

    def own_sum(g):
        net.arrived(("nearp", g))
        net.arrived(("nearm", g))
        own = gf.at[g, mine, block(0)]
        own[...] = (gh[g, :, block(0)].astype(F32) + near[g, 0].astype(F32) + near[g, 1].astype(F32)).astype(BF16)
        for name in ("yp", "ym", "twin"):
            net.send(("own" + name, g), own, own, to[name])

    def pass_on(g):
        net.arrived(("ownym", g))
        piece = gf.at[g, mine_part(0), block(1)]
        net.send(("passm", g), piece, piece, to["ym"])
        net.arrived(("ownyp", g))
        piece = gf.at[g, mine_part(1), block(3)]
        net.send(("passp", g), piece, piece, to["yp"])
        for dy in (1, 3):
            piece = gf.at[g, mine, block(dy)]
            net.send(("twin%d" % dy, g), piece, piece, to["twin"])

    def pass_far(g):
        net.arrived(("passm", g))
        net.arrived(("passp", g))
        piece = gf.at[g, mine, block(2)]
        net.send(("twin2", g), piece, piece, to["twin"])

    def product(g):
        for name in ("owntwin", "twin1", "twin3", "twin2"):
            net.arrived((name, g))
        if g == 1:
            net.arrived("pfp")
        if g == 3:
            net.arrived("pfm")
        if g == 0:
            net.arrived("pqp")
            net.arrived("pqm")

        @pl.loop(0, cols // 256)
        def _(n):
            at = pl.ds(pl.multiple_of(n * 256, 256), 256)
            acc = jnp.dot(gf[g], ax[:, at], preferred_element_type=F32)
            if g == 2:
                pb[2, :, at] = acc.astype(BF16)
            elif g == 1:
                pb[1, lo, at] = (acc[0:half] + pf[0, :, at].astype(F32)).astype(BF16)
                pb[1, hi, at] = acc[half:rows].astype(BF16)
            elif g == 3:
                pb[0, lo, at] = acc[0:half].astype(BF16)
                pb[0, hi, at] = (acc[half:rows] + pf[1, :, at].astype(F32)).astype(BF16)
            else:
                total = acc + (pq[0, :, at].astype(F32) + pq[1, :, at].astype(F32))
                new = 1.5 * w_ref[:, at] - 0.5 * total
                out_ref[:, at] = new
                outb_ref[:, at] = new.astype(BF16)

        if g == 2:
            net.send("pfp", pb.at[2, lo], pf.at[0], to["zp"])
            net.send("pfm", pb.at[2, hi], pf.at[1], to["zm"])
        elif g == 1:
            net.send("pqp", pb.at[1], pq.at[0], to["zp"])
        elif g == 3:
            net.send("pqm", pb.at[0], pq.at[1], to["zm"])

    stages = (partial_gram, chip_sum, far_sum, own_sum, pass_on, pass_far, product)
    for wave in range(len(GROUPS) + len(stages) - 1):
        for depth, stage in enumerate(stages):
            if 0 <= wave - depth < len(GROUPS):
                stage(GROUPS[wave - depth])
    net.drain()


def bjorck_step(w, wb):
    rows, cols = w.shape
    half, quarter, wide = rows // 2, rows // 4, rows * SIDE
    vmem = pl.BlockSpec(memory_space=pltpu.VMEM)
    copies = 12 + 4 * 13 + 4
    return pl.pallas_call(
        bjorck_kernel,
        name="bjorck_step",
        out_shape=(jax.ShapeDtypeStruct(w.shape, F32), jax.ShapeDtypeStruct(w.shape, BF16)),
        in_specs=[vmem, vmem],
        out_specs=(vmem, vmem),
        scratch_shapes=[
            pltpu.VMEM((SIDE, rows, cols), BF16),
            pltpu.VMEM((wide, cols), BF16),
            pltpu.VMEM((SIDE, rows, wide), BF16),
            pltpu.VMEM((SIDE, half, wide), BF16),
            pltpu.VMEM((SIDE, half, wide), BF16),
            pltpu.VMEM((SIDE, rows, wide), BF16),
            pltpu.VMEM((SIDE, 2, quarter, rows), BF16),
            pltpu.VMEM((SIDE, 2, half, rows), BF16),
            pltpu.VMEM((3, rows, cols), BF16),
            pltpu.VMEM((2, half, cols), BF16),
            pltpu.VMEM((2, rows, cols), BF16),
            pltpu.SemaphoreType.DMA((copies,)),
            pltpu.SemaphoreType.DMA((copies,)),
        ],
        compiler_params=pltpu.CompilerParams(
            collective_id=0, has_side_effects=True, vmem_limit_bytes=60 * 1024 * 1024
        ),
    )(w, wb)


def class_terms(logits, inner, norms_sq, row_labels):
    class_count = logits.shape[0]
    one_hot = (
        lax.broadcasted_iota(jnp.int32, (class_count, row_labels.shape[0]), 0)
        == row_labels[None, :]
    ).astype(jnp.float32)
    own_norm = jnp.sum(one_hot * norms_sq[:, None], axis=0)
    distance = own_norm[None, :] + norms_sq[:, None] - 2.0 * inner + 1e-05
    lipschitz = jnp.sqrt(jnp.where(one_hot > 0, 1.0, distance))
    plain_exp = jnp.exp(logits)
    bound_exp = (1.0 - one_hot) * jnp.exp(logits + lipschitz)
    partition = jnp.sum(plain_exp, axis=0) + jnp.sum(bound_exp, axis=0)
    row_loss = jnp.log(partition) - jnp.sum(one_hot * logits, axis=0)
    logit_grad = (plain_exp + bound_exp) / partition[None, :] - one_hot
    dist_grad = bound_exp / (partition[None, :] * 2.0 * lipschitz)
    return (row_loss, logit_grad, dist_grad)


def body(raw_weight, features, head, labels):
    pair = (((1,), (1,)), ((), ()))
    first_pair = (((0,), (0,)), ((), ()))
    current, weight_bf = raw_weight, raw_weight.astype(jnp.bfloat16)
    for _ in range(ITERS):
        current, weight_bf = bjorck_step(current, weight_bf)
    rows_in = features
    pre_sum = lax.psum_scatter(
        jnp.dot(rows_in, weight_bf, preferred_element_type=jnp.float32).astype(jnp.bfloat16),
        "row",
        scatter_dimension=0,
        tiled=True,
    ).astype(jnp.float32)
    activation = jnp.tanh(pre_sum)
    active_bf = activation.astype(jnp.bfloat16)
    class_count = head.shape[0]
    one_rows = (labels[:, None] == lax.broadcasted_iota(jnp.int32, (1, class_count), 1)).astype(
        jnp.bfloat16
    )
    picked = jnp.dot(one_rows, head, preferred_element_type=jnp.float32).astype(jnp.bfloat16)
    logit_part = lax.dot_general(head, active_bf, pair, preferred_element_type=jnp.float32)
    inner_part = lax.dot_general(head, picked, pair, preferred_element_type=jnp.float32)
    head_wide = head.astype(jnp.float32)
    norm_part = jnp.sum(head_wide * head_wide, axis=1)
    logits, inner, norms_sq = (
        lax.psum(logit_part.astype(jnp.bfloat16), "col").astype(jnp.float32),
        lax.psum(inner_part.astype(jnp.bfloat16), "col").astype(jnp.float32),
        lax.psum(norm_part.astype(jnp.bfloat16), "col").astype(jnp.float32),
    )
    row_loss, logit_grad, dist_grad = class_terms(logits, inner, norms_sq, labels)
    one_hot = (
        lax.broadcasted_iota(jnp.int32, (class_count, labels.shape[0]), 0) == labels[None, :]
    ).astype(jnp.float32)
    norm_grad = jnp.sum(dist_grad, axis=1) + jnp.sum(
        one_hot * jnp.sum(dist_grad, axis=0)[None, :], axis=1
    )
    highest = lax.Precision.HIGHEST
    label_side = lax.dot_general(dist_grad, head_wide, first_pair, precision=highest)
    head_term = (
        jnp.dot(logit_grad, active_bf.astype(jnp.float32), precision=highest)
        + 2.0 * norm_grad[:, None] * head_wide
        - 2.0 * jnp.dot(dist_grad, picked.astype(jnp.float32), precision=highest)
        - 2.0 * jnp.dot(one_hot, label_side, precision=highest)
    )
    head_grad = lax.psum(head_term.astype(jnp.bfloat16), "row").astype(jnp.float32)
    act_grad = lax.dot_general(logit_grad, head_wide, first_pair, precision=highest)
    pre_grad = (act_grad * (1.0 - activation * activation)).astype(jnp.bfloat16)
    rows_in = features
    weight_grad = lax.dot_general(
        rows_in,
        lax.all_gather(pre_grad, "row", axis=0, tiled=True),
        first_pair,
        preferred_element_type=jnp.float32,
    )
    return (current, row_loss, weight_grad, head_grad)


def solution(mesh):
    placed = (P("row", "col"), P(None, "row"), P(None, "col"), P("row"))
    return jax.shard_map(
        body,
        mesh=mesh,
        in_specs=placed,
        out_specs=(P("row", "col"), P("row"), P("row", "col"), P(None, "col")),
        check_vma=False,
    )
```

```python
import jax
import jax.numpy as jnp
from jax import lax
from jax.experimental import pallas as pl
from jax.experimental.pallas import tpu as pltpu
from jax.sharding import PartitionSpec as P

CLASSES = 100
ITERS = 2
SIDE = 4
F32 = jnp.float32
BF16 = jnp.bfloat16
MESH = pl.DeviceIdType.MESH
NT = (((1,), (1,)), ((), ()))


class Copies:
    def __init__(self, send_sems, recv_sems):
        self.sems = (send_sems, recv_sems)
        self.started = {}

    def send(self, name, src, dst, device):
        index = len(self.started)
        copy = pltpu.make_async_remote_copy(
            src_ref=src, dst_ref=dst, send_sem=self.sems[0].at[index], recv_sem=self.sems[1].at[index],
            device_id=device, device_id_type=MESH,
        )
        copy.start()
        self.started[name] = copy

    def arrived(self, name):
        self.started[name].wait_recv()

    def drain(self):
        for copy in self.started.values():
            copy.wait_send()


def neighbours():
    row, col = lax.axis_index("row"), lax.axis_index("col")
    x, z, y, core = row // SIDE, row % SIDE, col // 2, col % 2
    up = lambda v, d: (v + d) % SIDE
    return dict(
        zp=(x * SIDE + up(z, 1), col), zm=(x * SIDE + up(z, 3), col),
        xp=(up(x, 1) * SIDE + z, col), xm=(up(x, 3) * SIDE + z, col),
        yp=(row, up(y, 1) * 2 + core), ym=(row, up(y, 3) * 2 + core),
        twin=(row, y * 2 + 1 - core),
    )


def greet(devices):
    barrier = pltpu.get_barrier_semaphore()
    for device in devices:
        pl.semaphore_signal(barrier, inc=1, device_id=device, device_id_type=MESH)
    pl.semaphore_wait(barrier, len(devices))


GROUPS = (2, 1, 3, 0)


def bjorck_kernel(w_ref, wb_ref, out_ref, outb_ref, az, ax, gp, gr, gh, gf, far, near, pb, pf, pq, send_sems, recv_sems):
    rows, cols = w_ref.shape
    half, quarter, wide = rows // 2, rows // 4, rows * SIDE
    col = lax.axis_index("col")
    y, core = col // 2, col % 2
    to = neighbours()
    greet(list(to.values()))
    net = Copies(send_sems, recv_sems)
    mine = pl.ds(pl.multiple_of(core * half, half), half)
    other = pl.ds(pl.multiple_of((1 - core) * half, half), half)

    def mine_part(part):
        return pl.ds(pl.multiple_of(core * half + part * quarter, quarter), quarter)

    def block(dy):
        return pl.ds(pl.multiple_of(((y + dy) % SIDE) * rows, rows), rows)

    lo, hi = pl.ds(0, half), pl.ds(half, half)
    axrow = lambda d, part: pl.ds(d * rows + part * half, half)
    net.send("zm0", wb_ref.at[lo], az.at[1, lo], to["zm"])
    net.send("xm0", wb_ref.at[lo], ax.at[axrow(1, 0)], to["xm"])
    net.send("zp0", wb_ref.at[hi], az.at[3, hi], to["zp"])
    net.send("xp0", wb_ref.at[hi], ax.at[axrow(3, 1)], to["xp"])
    net.send("zm1", wb_ref.at[hi], az.at[1, hi], to["zm"])
    net.send("xm1", wb_ref.at[hi], ax.at[axrow(1, 1)], to["xm"])
    net.send("zp1", wb_ref.at[lo], az.at[3, lo], to["zp"])
    net.send("xp1", wb_ref.at[lo], ax.at[axrow(3, 0)], to["xp"])
    az[0] = wb_ref[...]
    ax[0:rows, :] = wb_ref[...]
    net.arrived("zm0")
    net.send("zm2", az.at[1, lo], az.at[2, lo], to["zm"])
    net.arrived("xm0")
    net.send("xm2", ax.at[axrow(1, 0)], ax.at[axrow(2, 0)], to["xm"])
    net.arrived("zp0")
    net.send("zp2", az.at[3, hi], az.at[2, hi], to["zp"])
    net.arrived("xp0")
    net.send("xp2", ax.at[axrow(3, 1)], ax.at[axrow(2, 1)], to["xp"])
    for name in ("zm1", "xm1", "zp1", "xp1", "zm2", "xm2", "zp2", "xp2"):
        net.arrived(name)

    def partial_gram(g):
        @pl.loop(0, wide // 512)
        def _(n):
            at = pl.ds(pl.multiple_of(n * 512, 512), 512)
            gp[g, :, at] = lax.dot_general(az[g], ax[at, :], NT, preferred_element_type=F32).astype(BF16)
        net.send(("twin", g), gp.at[g, other], gr.at[g], to["twin"])

    def chip_sum(g):
        net.arrived(("twin", g))
        gh[g] = (gp[g, mine].astype(F32) + gr[g].astype(F32)).astype(BF16)
        net.send(("farp", g), gh.at[g, 0:quarter, block(2)], far.at[g, 0], to["yp"])
        net.send(("farm", g), gh.at[g, quarter:half, block(2)], far.at[g, 1], to["ym"])

    def far_sum(g):
        net.arrived(("farp", g))
        one = gh.at[g, 0:quarter, block(1)]
        one[...] = (one[...].astype(F32) + far[g, 0].astype(F32)).astype(BF16)
        net.send(("nearp", g), gh.at[g, :, block(1)], near.at[g, 0], to["yp"])
        net.arrived(("farm", g))
        two = gh.at[g, quarter:half, block(3)]
        two[...] = (two[...].astype(F32) + far[g, 1].astype(F32)).astype(BF16)
        net.send(("nearm", g), gh.at[g, :, block(3)], near.at[g, 1], to["ym"])

    def own_sum(g):
        net.arrived(("nearp", g))
        net.arrived(("nearm", g))
        own = gf.at[g, mine, block(0)]
        own[...] = (gh[g, :, block(0)].astype(F32) + near[g, 0].astype(F32) + near[g, 1].astype(F32)).astype(BF16)
        for name in ("yp", "ym", "twin"):
            net.send(("own" + name, g), own, own, to[name])

    def pass_on(g):
        net.arrived(("ownym", g))
        piece = gf.at[g, mine_part(0), block(1)]
        net.send(("passm", g), piece, piece, to["ym"])
        net.arrived(("ownyp", g))
        piece = gf.at[g, mine_part(1), block(3)]
        net.send(("passp", g), piece, piece, to["yp"])
        for dy in (1, 3):
            piece = gf.at[g, mine, block(dy)]
            net.send(("twin%d" % dy, g), piece, piece, to["twin"])

    def pass_far(g):
        net.arrived(("passm", g))
        net.arrived(("passp", g))
        piece = gf.at[g, mine, block(2)]
        net.send(("twin2", g), piece, piece, to["twin"])

    def product(g):
        for name in ("owntwin", "twin1", "twin3", "twin2"):
            net.arrived((name, g))
        if g == 1:
            net.arrived("pfp")
        if g == 3:
            net.arrived("pfm")
        if g == 0:
            net.arrived("pqp")
            net.arrived("pqm")

        @pl.loop(0, cols // 256)
        def _(n):
            at = pl.ds(pl.multiple_of(n * 256, 256), 256)
            acc = jnp.dot(gf[g], ax[:, at], preferred_element_type=F32)
            if g == 2:
                pb[2, :, at] = acc.astype(BF16)
            elif g == 1:
                pb[1, lo, at] = (acc[0:half] + pf[0, :, at].astype(F32)).astype(BF16)
                pb[1, hi, at] = acc[half:rows].astype(BF16)
            elif g == 3:
                pb[0, lo, at] = acc[0:half].astype(BF16)
                pb[0, hi, at] = (acc[half:rows] + pf[1, :, at].astype(F32)).astype(BF16)
            else:
                total = acc + (pq[0, :, at].astype(F32) + pq[1, :, at].astype(F32))
                new = 1.5 * w_ref[:, at] - 0.5 * total
                out_ref[:, at] = new
                outb_ref[:, at] = new.astype(BF16)

        if g == 2:
            net.send("pfp", pb.at[2, lo], pf.at[0], to["zp"])
            net.send("pfm", pb.at[2, hi], pf.at[1], to["zm"])
        elif g == 1:
            net.send("pqp", pb.at[1], pq.at[0], to["zp"])
        elif g == 3:
            net.send("pqm", pb.at[0], pq.at[1], to["zm"])

    stages = (partial_gram, chip_sum, far_sum, own_sum, pass_on, pass_far, product)
    for wave in range(len(GROUPS) + len(stages) - 1):
        for depth, stage in enumerate(stages):
            if 0 <= wave - depth < len(GROUPS):
                stage(GROUPS[wave - depth])
    net.drain()


def bjorck_step(w, wb):
    rows, cols = w.shape
    half, quarter, wide = rows // 2, rows // 4, rows * SIDE
    vmem = pl.BlockSpec(memory_space=pltpu.VMEM)
    copies = 12 + 4 * 13 + 4
    return pl.pallas_call(
        bjorck_kernel,
        name="bjorck_step",
        out_shape=(jax.ShapeDtypeStruct(w.shape, F32), jax.ShapeDtypeStruct(w.shape, BF16)),
        in_specs=[vmem, vmem],
        out_specs=(vmem, vmem),
        scratch_shapes=[
            pltpu.VMEM((SIDE, rows, cols), BF16),
            pltpu.VMEM((wide, cols), BF16),
            pltpu.VMEM((SIDE, rows, wide), BF16),
            pltpu.VMEM((SIDE, half, wide), BF16),
            pltpu.VMEM((SIDE, half, wide), BF16),
            pltpu.VMEM((SIDE, rows, wide), BF16),
            pltpu.VMEM((SIDE, 2, quarter, rows), BF16),
            pltpu.VMEM((SIDE, 2, half, rows), BF16),
            pltpu.VMEM((3, rows, cols), BF16),
            pltpu.VMEM((2, half, cols), BF16),
            pltpu.VMEM((2, rows, cols), BF16),
            pltpu.SemaphoreType.DMA((copies,)),
            pltpu.SemaphoreType.DMA((copies,)),
        ],
        compiler_params=pltpu.CompilerParams(
            collective_id=0, has_side_effects=True, vmem_limit_bytes=60 * 1024 * 1024
        ),
    )(w, wb)


def gather_ring(net, name, piece, first, second, plus, minus):
    net.send((name, "p"), piece(0), piece(0), plus)
    net.send((name, "m"), piece(0), piece(0), minus)

    def finish():
        net.arrived((name, "m"))
        net.send((name, "fm"), first(1), first(1), minus)
        net.arrived((name, "p"))
        net.send((name, "fp"), second(3), second(3), plus)
        net.arrived((name, "fm"))
        net.arrived((name, "fp"))

    return finish


def add_to(ref, *terms):
    total = ref[...].astype(F32)
    for term in terms:
        total = total + term[...].astype(F32)
    ref[...] = total.astype(ref.dtype)


def tail_kernel(
    wb_ref, feat_ref, head_ref, labels_ref, loss_ref, wgrad_ref, hgrad_ref,
    pt, fa, na, fb, nb, sa, sb, f2a, n2a, f2b, n2b, kslots, lself, ltwin, lslots, act, pre, lgq, lgt, send_sems, recv_sems,
):
    row, col = lax.axis_index("row"), lax.axis_index("col")
    x, z, y, core = row // SIDE, row % SIDE, col // 2, col % 2
    toks = labels_ref.shape[1]
    hcols = wb_ref.shape[1] // 2
    tok2 = toks // 2
    at = lambda v, d: (v + d) % SIDE
    to = neighbours()
    peers = [(row, at(y, dy) * 2 + (core + dk) % 2) for dy in range(SIDE) for dk in range(2) if (dy, dk) != (0, 0)]
    greet([to["zp"], to["zm"], to["xp"], to["xm"]] + peers)
    net = Copies(send_sems, recv_sems)
    ca, cb = pl.ds(0, hcols), pl.ds(hcols, hcols)
    lo, hi = pl.ds(0, tok2), pl.ds(tok2, tok2)
    classes = head_ref.shape[0]

    kslots[col] = lax.dot_general(head_ref[...], head_ref[...], NT, preferred_element_type=F32)
    for peer, device in enumerate(peers):
        net.send(("k", peer), kslots.at[col], kslots.at[col], device)

    def forward(dx):
        start = pl.multiple_of(at(x, dx) * SIDE * toks, SIDE * toks)
        part = jnp.dot(feat_ref[pl.ds(start, SIDE * toks), :], wb_ref[...], preferred_element_type=F32)
        pt[dx] = part.astype(BF16).reshape(SIDE, toks, 2 * hcols)

    forward(2)
    net.send("fap", pt.at[2, 0:2, :, ca], fa.at[0], to["xp"])
    net.send("fam", pt.at[2, 2:4, :, ca], fa.at[1], to["xm"])
    forward(1)
    forward(3)
    forward(0)
    net.send("fbp", pt.at[0:2, at(z, 2), :, cb], fb.at[0], to["zp"])
    net.send("fbm", pt.at[2:4, at(z, 2), :, cb], fb.at[1], to["zm"])
    net.arrived("fap")
    add_to(pt.at[1, 0:2, :, ca], fa.at[0])
    net.send("nap", pt.at[1, :, :, ca], na.at[0], to["xp"])
    net.arrived("fam")
    add_to(pt.at[3, 2:4, :, ca], fa.at[1])
    net.send("nam", pt.at[3, :, :, ca], na.at[1], to["xm"])
    net.arrived("fbp")
    add_to(pt.at[0:2, at(z, 1), :, cb], fb.at[0])
    net.send("nbp", pt.at[:, at(z, 1), :, cb], nb.at[0], to["zp"])
    net.arrived("fbm")
    add_to(pt.at[2:4, at(z, 3), :, cb], fb.at[1])
    net.send("nbm", pt.at[:, at(z, 3), :, cb], nb.at[1], to["zm"])

    def sum_a(dz):
        zz = at(z, dz)
        return pt[0, zz, :, ca].astype(F32) + na[0, zz].astype(F32) + na[1, zz].astype(F32)

    def sum_b(dx):
        return pt[dx, z, :, cb].astype(F32) + nb[0, dx].astype(F32) + nb[1, dx].astype(F32)

    net.arrived("nap")
    net.arrived("nam")
    sa[2] = sum_a(2).astype(BF16)
    net.send("f2ap", sa.at[2, lo], f2a.at[0], to["zp"])
    net.send("f2am", sa.at[2, hi], f2a.at[1], to["zm"])
    sa[1] = sum_a(1).astype(BF16)
    sa[3] = sum_a(3).astype(BF16)
    net.arrived("nbp")
    net.arrived("nbm")
    sb[2] = sum_b(2).astype(BF16)
    net.send("f2bp", sb.at[2, lo], f2b.at[0], to["xp"])
    net.send("f2bm", sb.at[2, hi], f2b.at[1], to["xm"])
    sb[1] = sum_b(1).astype(BF16)
    sb[3] = sum_b(3).astype(BF16)
    net.arrived("f2ap")
    add_to(sa.at[1, lo], f2a.at[0])
    net.send("n2ap", sa.at[1], n2a.at[0], to["zp"])
    net.arrived("f2am")
    add_to(sa.at[3, hi], f2a.at[1])
    net.send("n2am", sa.at[3], n2a.at[1], to["zm"])
    net.arrived("f2bp")
    add_to(sb.at[1, lo], f2b.at[0])
    net.send("n2bp", sb.at[1], n2b.at[0], to["xp"])
    net.arrived("f2bm")
    add_to(sb.at[3, hi], f2b.at[1])
    net.send("n2bm", sb.at[3], n2b.at[1], to["xm"])
    own_a, own_b = sum_a(0), sum_b(0)
    net.arrived("n2ap")
    net.arrived("n2am")
    act[x, z, :, ca] = (own_a + n2a[0].astype(F32) + n2a[1].astype(F32)).astype(BF16)
    net.arrived("n2bp")
    net.arrived("n2bm")
    act[x, z, :, cb] = (own_b + n2b[0].astype(F32) + n2b[1].astype(F32)).astype(BF16)

    ga = gather_ring(
        net, "ga", lambda d: act.at[at(x, d), z, :, ca], lambda d: act.at[at(x, d), z, lo, ca],
        lambda d: act.at[at(x, d), z, hi, ca], to["xp"], to["xm"],
    )
    gb = gather_ring(
        net, "gb", lambda d: act.at[x, at(z, d), :, cb], lambda d: act.at[x, at(z, d), lo, cb],
        lambda d: act.at[x, at(z, d), hi, cb], to["zp"], to["zm"],
    )
    own_act = jnp.tanh(act[x, z].astype(F32)).astype(BF16)
    lself[...] = lax.dot_general(head_ref[...], own_act, NT, preferred_element_type=F32)
    net.send("ltwin", lself, ltwin, to["twin"])
    ga()
    g2a = gather_ring(
        net, "g2a", lambda d: act.at[:, at(z, d), :, ca], lambda d: act.at[0:2, at(z, d), :, ca],
        lambda d: act.at[2:4, at(z, d), :, ca], to["zp"], to["zm"],
    )
    gb()
    g2b = gather_ring(
        net, "g2b", lambda d: act.at[at(x, d), :, :, cb], lambda d: act.at[at(x, d), 0:2, :, cb],
        lambda d: act.at[at(x, d), 2:4, :, cb], to["xp"], to["xm"],
    )
    net.arrived("ltwin")
    lslots[y] = (lself[...] + ltwin[...]).astype(BF16)
    for dy in (1, 2, 3):
        net.send(("l", dy), lslots.at[y], lslots.at[y], (row, at(y, dy) * 2 + core))

    for peer in range(len(peers)):
        net.arrived(("k", peer))
    pair_products = kslots[0]
    for other in range(1, 2 * SIDE):
        pair_products = pair_products + kslots[other]
    ids = lax.broadcasted_iota(jnp.int32, (classes, classes), 0)
    eye = ids == lax.broadcasted_iota(jnp.int32, (classes, classes), 1)
    class_ids = lax.broadcasted_iota(jnp.int32, (classes, toks), 0)
    one_hot = (class_ids == labels_ref[...]).astype(F32)
    high = lax.Precision.HIGHEST
    norms = jnp.sum(jnp.where(eye, pair_products, 0.0), axis=1, keepdims=True)
    inner = jnp.dot(pair_products, one_hot, precision=high, preferred_element_type=F32)
    own_norm = jnp.sum(one_hot * norms, axis=0, keepdims=True)
    distance = own_norm + norms - 2.0 * inner + 1e-05
    lipschitz = jnp.sqrt(jnp.where(one_hot > 0, 1.0, distance))

    for dy in (1, 2, 3):
        net.arrived(("l", dy))
    logits = lslots[0].astype(F32)
    for other in range(1, SIDE):
        logits = logits + lslots[other].astype(F32)
    real = (class_ids < CLASSES).astype(F32)
    plain_exp = real * jnp.exp(logits)
    bound_exp = (real - one_hot) * jnp.exp(logits + lipschitz)
    partition = jnp.sum(plain_exp, axis=0, keepdims=True) + jnp.sum(bound_exp, axis=0, keepdims=True)
    loss_ref[...] = jnp.log(partition) - jnp.sum(one_hot * logits, axis=0, keepdims=True)
    logit_grad = (plain_exp + bound_exp) / partition - one_hot
    dist_grad = bound_exp / (partition * 2.0 * lipschitz)
    lgq[x, z] = logit_grad.astype(BF16)
    pairs = lax.dot_general(one_hot, dist_grad, NT, precision=high, preferred_element_type=F32)
    pairs = pairs + lax.dot_general(dist_grad, one_hot, NT, precision=high, preferred_element_type=F32)
    lgt[x, z] = pairs.astype(BF16)
    cl, ch = pl.ds(0, classes // 2), pl.ds(classes // 2, classes // 2)
    gl = gather_ring(
        net, "gl", lambda d: lgq.at[at(x, d), z], lambda d: lgq.at[at(x, d), z, cl],
        lambda d: lgq.at[at(x, d), z, ch], to["xp"], to["xm"],
    )
    gt = gather_ring(
        net, "gt", lambda d: lgt.at[x, at(z, d)], lambda d: lgt.at[x, at(z, d), cl],
        lambda d: lgt.at[x, at(z, d), ch], to["zp"], to["zm"],
    )
    gl()
    g2l = gather_ring(
        net, "g2l", lambda d: lgq.at[:, at(z, d)], lambda d: lgq.at[0:2, at(z, d)],
        lambda d: lgq.at[2:4, at(z, d)], to["zp"], to["zm"],
    )
    gt()
    g2t = gather_ring(
        net, "g2t", lambda d: lgt.at[at(x, d)], lambda d: lgt.at[at(x, d), 0:2],
        lambda d: lgt.at[at(x, d), 2:4], to["xp"], to["xm"],
    )
    g2a()
    g2b()
    g2l()
    g2t()

    total = jnp.zeros((classes, classes), F32)
    for block in range(SIDE * SIDE):
        total = total + lgt[block // SIDE, block % SIDE].astype(F32)
    laplace = jnp.where(eye, jnp.sum(total, axis=1, keepdims=True), 0.0) - total
    hgrad_ref[...] = 2.0 * jnp.dot(laplace, head_ref[...].astype(F32), precision=high, preferred_element_type=F32)

    first_pair = (((0,), (0,)), ((), ()))

    @pl.loop(0, SIDE * SIDE)
    def _(block):
        bx, bz = block // SIDE, block % SIDE
        tokens = pl.ds(pl.multiple_of(block * toks, toks), toks)
        grads = lgq[bx, bz]
        active = jnp.tanh(act[bx, bz].astype(F32))
        act_grad = lax.dot_general(grads, head_ref[...], first_pair, preferred_element_type=F32)
        pre_grad = (act_grad * (1.0 - active * active)).astype(BF16)
        pre[tokens, :] = pre_grad
        hgrad_ref[...] += jnp.dot(grads, active.astype(BF16), preferred_element_type=F32)

    @pl.loop(0, 3)
    def _(n):
        cols = pl.ds(pl.multiple_of(n * 256, 256), 256)
        wgrad_ref[:, cols] = lax.dot_general(feat_ref[...], pre[:, cols], first_pair, preferred_element_type=F32)

    net.drain()


def tail(wb, features, head, labels):
    toks, width = labels.shape[0], head.shape[1]
    hcols, tok2 = width // 2, toks // 2
    classes = 128
    padded = jnp.pad(head, ((0, classes - head.shape[0]), (0, 0)))
    vmem = pl.BlockSpec(memory_space=pltpu.VMEM)
    copies = 7 + 16 + 4 * 8 + 1 + 3
    loss, wgrad, hgrad = pl.pallas_call(
        tail_kernel,
        name="tail",
        out_shape=(
            jax.ShapeDtypeStruct((1, toks), F32),
            jax.ShapeDtypeStruct((features.shape[1], width), F32),
            jax.ShapeDtypeStruct((classes, width), F32),
        ),
        in_specs=[vmem] * 4,
        out_specs=(vmem,) * 3,
        scratch_shapes=[
            pltpu.VMEM((SIDE, SIDE, toks, width), BF16),
            pltpu.VMEM((2, 2, toks, hcols), BF16),
            pltpu.VMEM((2, SIDE, toks, hcols), BF16),
            pltpu.VMEM((2, 2, toks, hcols), BF16),
            pltpu.VMEM((2, SIDE, toks, hcols), BF16),
            pltpu.VMEM((SIDE, toks, hcols), BF16),
            pltpu.VMEM((SIDE, toks, hcols), BF16),
            pltpu.VMEM((2, tok2, hcols), BF16),
            pltpu.VMEM((2, toks, hcols), BF16),
            pltpu.VMEM((2, tok2, hcols), BF16),
            pltpu.VMEM((2, toks, hcols), BF16),
            pltpu.VMEM((2 * SIDE, classes, classes), F32),
            pltpu.VMEM((classes, toks), F32),
            pltpu.VMEM((classes, toks), F32),
            pltpu.VMEM((SIDE, classes, toks), BF16),
            pltpu.VMEM((SIDE, SIDE, toks, width), BF16),
            pltpu.VMEM((SIDE * SIDE * toks, width), BF16),
            pltpu.VMEM((SIDE, SIDE, classes, toks), BF16),
            pltpu.VMEM((SIDE, SIDE, classes, classes), BF16),
            pltpu.SemaphoreType.DMA((copies,)),
            pltpu.SemaphoreType.DMA((copies,)),
        ],
        compiler_params=pltpu.CompilerParams(
            collective_id=1, has_side_effects=True, vmem_limit_bytes=60 * 1024 * 1024
        ),
    )(wb, features, padded, labels.reshape(1, toks))
    return loss.reshape(toks), wgrad, hgrad[: head.shape[0]]


def body(raw_weight, features, head, labels):
    current, weight_bf = raw_weight, raw_weight.astype(BF16)
    for _ in range(ITERS):
        current, weight_bf = bjorck_step(current, weight_bf)
    row_loss, weight_grad, head_grad = tail(weight_bf, features, head, labels)
    return (current, row_loss, weight_grad, head_grad)


def solution(mesh):
    placed = (P("row", "col"), P(None, "row"), P(None, "col"), P("row"))
    return jax.shard_map(
        body,
        mesh=mesh,
        in_specs=placed,
        out_specs=(P("row", "col"), P("row"), P("row", "col"), P(None, "col")),
        check_vma=False,
    )
```

```python
import jax
import jax.numpy as jnp
from jax import lax
from jax.experimental import pallas as pl
from jax.experimental.pallas import tpu as pltpu
from jax.sharding import PartitionSpec as P

CLASSES = 100
ITERS = 2
SIDE = 4
F32 = jnp.float32
BF16 = jnp.bfloat16
MESH = pl.DeviceIdType.MESH
NT = (((1,), (1,)), ((), ()))
TN = (((0,), (0,)), ((), ()))


class Copies:
    def __init__(self, send_sems, recv_sems):
        self.sems = (send_sems, recv_sems)
        self.started = {}

    def send(self, name, src, dst, device):
        index = len(self.started)
        copy = pltpu.make_async_remote_copy(
            src_ref=src, dst_ref=dst, send_sem=self.sems[0].at[index], recv_sem=self.sems[1].at[index],
            device_id=device, device_id_type=MESH,
        )
        copy.start()
        self.started[name] = copy

    def arrived(self, name):
        self.started[name].wait_recv()

    def drain(self):
        for copy in self.started.values():
            copy.wait_send()


def neighbours():
    row, col = lax.axis_index("row"), lax.axis_index("col")
    x, z, y, core = row // SIDE, row % SIDE, col // 2, col % 2
    up = lambda v, d: (v + d) % SIDE
    return dict(
        zp=(x * SIDE + up(z, 1), col), zm=(x * SIDE + up(z, 3), col),
        xp=(up(x, 1) * SIDE + z, col), xm=(up(x, 3) * SIDE + z, col),
        yp=(row, up(y, 1) * 2 + core), ym=(row, up(y, 3) * 2 + core),
        twin=(row, y * 2 + 1 - core),
    )


def greet(devices):
    barrier = pltpu.get_barrier_semaphore()
    for device in devices:
        pl.semaphore_signal(barrier, inc=1, device_id=device, device_id_type=MESH)
    pl.semaphore_wait(barrier, len(devices))


def add_to(ref, *terms):
    total = ref[...].astype(F32)
    for term in terms:
        total = total + term[...].astype(F32)
    ref[...] = total.astype(ref.dtype)


PAIRS = (((1, 1), (0, 1)), ((1, 2), (2, 1)), ((2, 2), (1, 3)), ((1, 0), (0, 0)), ((2, 0), (0, 2)))
WHERE = {offset: (pair, which) for pair, both in enumerate(PAIRS) for which, offset in enumerate(both)}


def bjorck_kernel(
    w_ref, out_ref, az, ax, gp, gr, gh, gf, far, near, px1, px2, px3, pz1, pz2, pfx, pqx, pfz, pqz, zr1, zr2, send_sems, recv_sems
):
    rows, cols = w_ref.shape
    half, quarter, eighth, third = rows // 2, rows // 4, rows // 8, rows // 3
    col = lax.axis_index("col")
    y, core = col // 2, col % 2
    to = neighbours()
    greet(list(to.values()))
    net = Copies(send_sems, recv_sems)

    def block(dy, part=None):
        start = ((y + dy) % SIDE) * quarter
        if part is None:
            return pl.ds(pl.multiple_of(start, quarter), quarter)
        return pl.ds(pl.multiple_of(start + part * eighth, eighth), eighth)

    lo, hi = pl.ds(0, half), pl.ds(half, half)
    top, rest = pl.ds(0, third), pl.ds(third, rows - third)
    az[0] = w_ref[...].astype(BF16)
    own = az.at[0]
    net.send("zm0", own.at[top], az.at[1, top], to["zm"])
    net.send("xm0", own.at[lo], ax.at[1, lo], to["xm"])
    net.send("zp0", own.at[rest], az.at[3, rest], to["zp"])
    net.send("xp0", own.at[hi], ax.at[3, hi], to["xp"])
    net.send("zm1", own.at[rest], az.at[1, rest], to["zm"])
    net.send("xm1", own.at[hi], ax.at[1, hi], to["xm"])
    net.send("xp1", own.at[lo], ax.at[3, lo], to["xp"])
    ax[0] = az[0]
    net.arrived("zm0")
    net.send("zm2", az.at[1, top], az.at[2, top], to["zm"])
    net.arrived("xm0")
    net.send("xm2", ax.at[1, lo], ax.at[2, lo], to["xm"])
    net.arrived("xp0")
    net.send("xp2", ax.at[3, hi], ax.at[2, hi], to["xp"])
    net.arrived("zp0")
    net.send("zp2", az.at[3, rest], az.at[2, rest], to["zp"])
    needs = {0: ("zm1", "xm1"), 1: ("xm2", "xp2", "zm2", "zp2"), 2: ("xp1",), 3: (), 4: ()}

    def partial_gram(p):
        for name in needs[p]:
            net.arrived(name)
        for which, (dz, dx) in enumerate(PAIRS[p]):
            gp[p, which] = lax.dot_general(az[dz], ax[dx], NT, preferred_element_type=F32).astype(BF16)
        net.send(("twin", p), gp.at[p, 1 - core], gr.at[p], to["twin"])

    def chip_sum(p):
        net.arrived(("twin", p))
        gh[p] = (gp[p, core].astype(F32) + gr[p].astype(F32)).astype(BF16)
        net.send(("farp", p), gh.at[p, block(2, 0)], far.at[p, 0], to["yp"])
        net.send(("farm", p), gh.at[p, block(2, 1)], far.at[p, 1], to["ym"])

    def far_sum(p):
        net.arrived(("farp", p))
        add_to(gh.at[p, block(1, 0)], far.at[p, 0])
        net.send(("nearp", p), gh.at[p, block(1)], near.at[p, 0], to["yp"])
        net.arrived(("farm", p))
        add_to(gh.at[p, block(3, 1)], far.at[p, 1])
        net.send(("nearm", p), gh.at[p, block(3)], near.at[p, 1], to["ym"])

    def own_sum(p):
        net.arrived(("nearp", p))
        net.arrived(("nearm", p))
        piece = gf.at[p, core, block(0)]
        piece[...] = (gh[p, block(0)].astype(F32) + near[p, 0].astype(F32) + near[p, 1].astype(F32)).astype(BF16)
        for name in ("yp", "ym", "twin"):
            net.send(("own" + name, p), piece, piece, to[name])

    def pass_on(p):
        net.arrived(("ownym", p))
        piece = gf.at[p, core, block(1, 0)]
        net.send(("passm", p), piece, piece, to["ym"])
        net.arrived(("ownyp", p))
        piece = gf.at[p, core, block(3, 1)]
        net.send(("passp", p), piece, piece, to["yp"])
        for dy in (1, 3):
            piece = gf.at[p, core, block(dy)]
            net.send(("twin%d" % dy, p), piece, piece, to["twin"])

    def pass_far(p):
        net.arrived(("passm", p))
        net.arrived(("passp", p))
        piece = gf.at[p, core, block(2)]
        net.send(("twin2", p), piece, piece, to["twin"])

    def ready(p):
        for name in ("owntwin", "twin1", "twin3", "twin2"):
            net.arrived((name, p))

    def combine(direct, mirrored, put):
        @pl.loop(0, cols // 256)
        def _(n):
            at = pl.ds(pl.multiple_of(n * 256, 256), 256)
            acc = None
            for dz, dx in direct:
                term = jnp.dot(gf[WHERE[dz, dx]], ax[dx, :, at], preferred_element_type=F32)
                acc = term if acc is None else acc + term
            for dz, dx in mirrored:
                term = lax.dot_general(gf[WHERE[dz, dx]], az[dz, :, at], TN, preferred_element_type=F32)
                acc = term if acc is None else acc + term
            put(at, acc)

    def store(ref):
        def put(at, acc):
            ref[:, at] = acc.astype(BF16)
        return put

    def after_one():
        ready(0)
        ready(1)
        combine([], [(1, 2)], store(px2))
        net.send("x2p", px2.at[lo], pfx.at[0], to["xp"])
        net.send("x2m", px2.at[hi], pfx.at[1], to["xm"])
        combine([], [(1, 1), (2, 1), (0, 1)], store(px1))

    def after_two():
        ready(2)
        combine([(2, 1), (2, 2)], [], store(pz2))
        net.send("z2m", pz2.at[rest], zr1, to["zm"])
        net.send("z2p", pz2.at[top], pfz, to["zp"])
        net.arrived("x2p")
        add_to(px1.at[lo], pfx.at[0])
        net.send("x1", px1, pqx.at[0], to["xp"])
        combine([], [(1, 3)], store(px3))
        net.arrived("x2m")
        add_to(px3.at[hi], pfx.at[1])
        net.send("x3", px3, pqx.at[1], to["xm"])

    def after_three():
        ready(3)
        net.arrived("z2m")
        net.send("z2r", zr1, zr2, to["zm"])
        combine([(1, 0), (1, 1), (1, 2), (1, 3)], [], store(pz1))
        net.arrived("z2p")
        add_to(pz1.at[top], pfz)
        net.send("z1", pz1, pqz, to["zp"])

    def after_four():
        ready(4)

        def put(at, acc):
            out_ref[:, at] = 1.5 * w_ref[:, at] - 0.5 * acc

        combine([(0, 0), (0, 1), (0, 2)], [(1, 0), (2, 0)], put)
        for name in ("x1", "x3", "z2r", "z1"):
            net.arrived(name)
        out_ref[top] -= 0.5 * (pqx[0, top].astype(F32) + pqx[1, top].astype(F32) + pqz[top].astype(F32))
        out_ref[rest] -= 0.5 * (
            pqx[0, rest].astype(F32) + pqx[1, rest].astype(F32) + pqz[rest].astype(F32) + zr2[...].astype(F32)
        )

    def run(*steps):
        for stage, p in steps:
            (partial_gram, chip_sum, far_sum, own_sum, pass_on, pass_far)[stage](p)

    run((0, 0), (1, 0), (2, 0), (0, 1))
    run((3, 0), (1, 1), (0, 2))
    run((4, 0), (2, 1), (1, 2), (0, 3))
    run((5, 0), (3, 1), (2, 2), (1, 3), (0, 4))
    run((4, 1), (3, 2), (2, 3), (1, 4))
    run((5, 1), (4, 2), (3, 3), (2, 4))
    after_one()
    run((5, 2), (4, 3), (3, 4))
    after_two()
    run((5, 3), (4, 4))
    after_three()
    run((5, 4))
    after_four()
    net.drain()


def bjorck_step(w):
    rows, cols = w.shape
    vmem = pl.BlockSpec(memory_space=pltpu.VMEM)
    pairs, copies = len(PAIRS), 11 + 13 * len(PAIRS) + 8
    part = lambda *shape: pltpu.VMEM(shape, BF16)
    return pl.pallas_call(
        bjorck_kernel,
        name="bjorck_step",
        out_shape=jax.ShapeDtypeStruct(w.shape, F32),
        in_specs=[vmem],
        out_specs=vmem,
        scratch_shapes=[
            part(SIDE, rows, cols),
            part(SIDE, rows, cols),
            part(pairs, 2, rows, rows),
            part(pairs, rows, rows),
            part(pairs, rows, rows),
            part(pairs, 2, rows, rows),
            part(pairs, 2, rows // 8, rows),
            part(pairs, 2, rows // 4, rows),
            part(rows, cols),
            part(rows, cols),
            part(rows, cols),
            part(rows, cols),
            part(rows, cols),
            part(2, rows // 2, cols),
            part(2, rows, cols),
            part(rows // 3, cols),
            part(rows, cols),
            part(rows - rows // 3, cols),
            part(rows - rows // 3, cols),
            pltpu.SemaphoreType.DMA((copies,)),
            pltpu.SemaphoreType.DMA((copies,)),
        ],
        compiler_params=pltpu.CompilerParams(
            collective_id=0, has_side_effects=True, vmem_limit_bytes=60 * 1024 * 1024
        ),
    )(w)


def gather_ring(net, name, piece, first, second, plus, minus):
    net.send((name, "p"), piece(0), piece(0), plus)
    net.send((name, "m"), piece(0), piece(0), minus)

    def finish():
        net.arrived((name, "m"))
        net.send((name, "fm"), first(1), first(1), minus)
        net.arrived((name, "p"))
        net.send((name, "fp"), second(3), second(3), plus)
        net.arrived((name, "fm"))
        net.arrived((name, "fp"))

    return finish


def tail_kernel(
    w_ref, feat_ref, head_ref, labels_ref, loss_ref, wgrad_ref, hgrad_ref,
    wb, pt, fa, na, fb, nb, sa, sb, f2a, n2a, f2b, n2b, kslots, lself, ltwin, lslots, act, pre, lgq, lgt, send_sems, recv_sems,
):
    row, col = lax.axis_index("row"), lax.axis_index("col")
    x, z, y, core = row // SIDE, row % SIDE, col // 2, col % 2
    toks = labels_ref.shape[1]
    hcols = w_ref.shape[1] // 2
    tok2 = toks // 2
    at = lambda v, d: (v + d) % SIDE
    to = neighbours()
    peers = [(row, at(y, dy) * 2 + (core + dk) % 2) for dy in range(SIDE) for dk in range(2) if (dy, dk) != (0, 0)]
    greet([to["zp"], to["zm"], to["xp"], to["xm"]] + peers)
    net = Copies(send_sems, recv_sems)
    ca, cb = pl.ds(0, hcols), pl.ds(hcols, hcols)
    lo, hi = pl.ds(0, tok2), pl.ds(tok2, tok2)
    classes = head_ref.shape[0]

    kslots[col] = lax.dot_general(head_ref[...], head_ref[...], NT, preferred_element_type=F32)
    for peer, device in enumerate(peers):
        net.send(("k", peer), kslots.at[col], kslots.at[col], device)

    wb[...] = w_ref[...].astype(BF16)
    def forward(dx):
        start = pl.multiple_of(at(x, dx) * SIDE * toks, SIDE * toks)
        part = jnp.dot(feat_ref[pl.ds(start, SIDE * toks), :], wb[...], preferred_element_type=F32)
        pt[dx] = part.astype(BF16).reshape(SIDE, toks, 2 * hcols)

    forward(2)
    net.send("fap", pt.at[2, 0:2, :, ca], fa.at[0], to["xp"])
    net.send("fam", pt.at[2, 2:4, :, ca], fa.at[1], to["xm"])
    forward(1)
    forward(3)
    forward(0)
    net.send("fbp", pt.at[0:2, at(z, 2), :, cb], fb.at[0], to["zp"])
    net.send("fbm", pt.at[2:4, at(z, 2), :, cb], fb.at[1], to["zm"])
    net.arrived("fap")
    add_to(pt.at[1, 0:2, :, ca], fa.at[0])
    net.send("nap", pt.at[1, :, :, ca], na.at[0], to["xp"])
    net.arrived("fam")
    add_to(pt.at[3, 2:4, :, ca], fa.at[1])
    net.send("nam", pt.at[3, :, :, ca], na.at[1], to["xm"])
    net.arrived("fbp")
    add_to(pt.at[0:2, at(z, 1), :, cb], fb.at[0])
    net.send("nbp", pt.at[:, at(z, 1), :, cb], nb.at[0], to["zp"])
    net.arrived("fbm")
    add_to(pt.at[2:4, at(z, 3), :, cb], fb.at[1])
    net.send("nbm", pt.at[:, at(z, 3), :, cb], nb.at[1], to["zm"])

    def sum_a(dz):
        zz = at(z, dz)
        return pt[0, zz, :, ca].astype(F32) + na[0, zz].astype(F32) + na[1, zz].astype(F32)

    def sum_b(dx):
        return pt[dx, z, :, cb].astype(F32) + nb[0, dx].astype(F32) + nb[1, dx].astype(F32)

    net.arrived("nap")
    net.arrived("nam")
    sa[2] = sum_a(2).astype(BF16)
    net.send("f2ap", sa.at[2, lo], f2a.at[0], to["zp"])
    net.send("f2am", sa.at[2, hi], f2a.at[1], to["zm"])
    sa[1] = sum_a(1).astype(BF16)
    sa[3] = sum_a(3).astype(BF16)
    net.arrived("nbp")
    net.arrived("nbm")
    sb[2] = sum_b(2).astype(BF16)
    net.send("f2bp", sb.at[2, lo], f2b.at[0], to["xp"])
    net.send("f2bm", sb.at[2, hi], f2b.at[1], to["xm"])
    sb[1] = sum_b(1).astype(BF16)
    sb[3] = sum_b(3).astype(BF16)
    net.arrived("f2ap")
    add_to(sa.at[1, lo], f2a.at[0])
    net.send("n2ap", sa.at[1], n2a.at[0], to["zp"])
    net.arrived("f2am")
    add_to(sa.at[3, hi], f2a.at[1])
    net.send("n2am", sa.at[3], n2a.at[1], to["zm"])
    net.arrived("f2bp")
    add_to(sb.at[1, lo], f2b.at[0])
    net.send("n2bp", sb.at[1], n2b.at[0], to["xp"])
    net.arrived("f2bm")
    add_to(sb.at[3, hi], f2b.at[1])
    net.send("n2bm", sb.at[3], n2b.at[1], to["xm"])
    own_a, own_b = sum_a(0), sum_b(0)
    net.arrived("n2ap")
    net.arrived("n2am")
    act[x, z, :, ca] = (own_a + n2a[0].astype(F32) + n2a[1].astype(F32)).astype(BF16)
    net.arrived("n2bp")
    net.arrived("n2bm")
    act[x, z, :, cb] = (own_b + n2b[0].astype(F32) + n2b[1].astype(F32)).astype(BF16)

    ga = gather_ring(
        net, "ga", lambda d: act.at[at(x, d), z, :, ca], lambda d: act.at[at(x, d), z, lo, ca],
        lambda d: act.at[at(x, d), z, hi, ca], to["xp"], to["xm"],
    )
    gb = gather_ring(
        net, "gb", lambda d: act.at[x, at(z, d), :, cb], lambda d: act.at[x, at(z, d), lo, cb],
        lambda d: act.at[x, at(z, d), hi, cb], to["zp"], to["zm"],
    )
    own_act = jnp.tanh(act[x, z].astype(F32)).astype(BF16)
    lself[...] = lax.dot_general(head_ref[...], own_act, NT, preferred_element_type=F32)
    net.send("ltwin", lself, ltwin, to["twin"])
    ga()
    g2a = gather_ring(
        net, "g2a", lambda d: act.at[:, at(z, d), :, ca], lambda d: act.at[0:2, at(z, d), :, ca],
        lambda d: act.at[2:4, at(z, d), :, ca], to["zp"], to["zm"],
    )
    gb()
    g2b = gather_ring(
        net, "g2b", lambda d: act.at[at(x, d), :, :, cb], lambda d: act.at[at(x, d), 0:2, :, cb],
        lambda d: act.at[at(x, d), 2:4, :, cb], to["xp"], to["xm"],
    )
    net.arrived("ltwin")
    lslots[y] = (lself[...] + ltwin[...]).astype(BF16)
    for dy in (1, 2, 3):
        net.send(("l", dy), lslots.at[y], lslots.at[y], (row, at(y, dy) * 2 + core))

    for peer in range(len(peers)):
        net.arrived(("k", peer))
    pair_products = kslots[0]
    for other in range(1, 2 * SIDE):
        pair_products = pair_products + kslots[other]
    ids = lax.broadcasted_iota(jnp.int32, (classes, classes), 0)
    eye = ids == lax.broadcasted_iota(jnp.int32, (classes, classes), 1)
    class_ids = lax.broadcasted_iota(jnp.int32, (classes, toks), 0)
    one_hot = (class_ids == labels_ref[...]).astype(F32)
    high = lax.Precision.HIGHEST
    norms = jnp.sum(jnp.where(eye, pair_products, 0.0), axis=1, keepdims=True)
    inner = jnp.dot(pair_products, one_hot, precision=high, preferred_element_type=F32)
    own_norm = jnp.sum(one_hot * norms, axis=0, keepdims=True)
    distance = own_norm + norms - 2.0 * inner + 1e-05
    lipschitz = jnp.sqrt(jnp.where(one_hot > 0, 1.0, distance))

    for dy in (1, 2, 3):
        net.arrived(("l", dy))
    logits = lslots[0].astype(F32)
    for other in range(1, SIDE):
        logits = logits + lslots[other].astype(F32)
    real = (class_ids < CLASSES).astype(F32)
    plain_exp = real * jnp.exp(logits)
    bound_exp = (real - one_hot) * jnp.exp(logits + lipschitz)
    partition = jnp.sum(plain_exp, axis=0, keepdims=True) + jnp.sum(bound_exp, axis=0, keepdims=True)
    loss_ref[...] = jnp.log(partition) - jnp.sum(one_hot * logits, axis=0, keepdims=True)
    logit_grad = (plain_exp + bound_exp) / partition - one_hot
    dist_grad = bound_exp / (partition * 2.0 * lipschitz)
    lgq[x, z] = logit_grad.astype(BF16)
    pairs = lax.dot_general(one_hot, dist_grad, NT, precision=high, preferred_element_type=F32)
    pairs = pairs + lax.dot_general(dist_grad, one_hot, NT, precision=high, preferred_element_type=F32)
    lgt[x, z] = pairs.astype(BF16)
    cl, ch = pl.ds(0, classes // 2), pl.ds(classes // 2, classes // 2)
    gl = gather_ring(
        net, "gl", lambda d: lgq.at[at(x, d), z], lambda d: lgq.at[at(x, d), z, cl],
        lambda d: lgq.at[at(x, d), z, ch], to["xp"], to["xm"],
    )
    gt = gather_ring(
        net, "gt", lambda d: lgt.at[x, at(z, d)], lambda d: lgt.at[x, at(z, d), cl],
        lambda d: lgt.at[x, at(z, d), ch], to["zp"], to["zm"],
    )
    gl()
    g2l = gather_ring(
        net, "g2l", lambda d: lgq.at[:, at(z, d)], lambda d: lgq.at[0:2, at(z, d)],
        lambda d: lgq.at[2:4, at(z, d)], to["zp"], to["zm"],
    )
    gt()
    g2t = gather_ring(
        net, "g2t", lambda d: lgt.at[at(x, d)], lambda d: lgt.at[at(x, d), 0:2],
        lambda d: lgt.at[at(x, d), 2:4], to["xp"], to["xm"],
    )
    g2a()
    g2b()
    g2l()
    g2t()

    total = jnp.zeros((classes, classes), F32)
    for block in range(SIDE * SIDE):
        total = total + lgt[block // SIDE, block % SIDE].astype(F32)
    laplace = jnp.where(eye, jnp.sum(total, axis=1, keepdims=True), 0.0) - total
    hgrad_ref[...] = 2.0 * jnp.dot(laplace, head_ref[...].astype(F32), precision=high, preferred_element_type=F32)

    @pl.loop(0, SIDE * SIDE)
    def _(block):
        bx, bz = block // SIDE, block % SIDE
        tokens = pl.ds(pl.multiple_of(block * toks, toks), toks)
        grads = lgq[bx, bz]
        active = jnp.tanh(act[bx, bz].astype(F32))
        act_grad = lax.dot_general(grads, head_ref[...], TN, preferred_element_type=F32)
        pre_grad = (act_grad * (1.0 - active * active)).astype(BF16)
        pre[tokens, :] = pre_grad
        hgrad_ref[...] += jnp.dot(grads, active.astype(BF16), preferred_element_type=F32)

    @pl.loop(0, 3)
    def _(n):
        cols = pl.ds(pl.multiple_of(n * 256, 256), 256)
        wgrad_ref[:, cols] = lax.dot_general(feat_ref[...], pre[:, cols], TN, preferred_element_type=F32)

    net.drain()


def tail(w, features, head, labels):
    toks, width = labels.shape[0], head.shape[1]
    hcols, tok2 = width // 2, toks // 2
    classes = 128
    padded = jnp.pad(head, ((0, classes - head.shape[0]), (0, 0)))
    vmem = pl.BlockSpec(memory_space=pltpu.VMEM)
    copies = 7 + 16 + 4 * 8 + 1 + 3
    loss, wgrad, hgrad = pl.pallas_call(
        tail_kernel,
        name="tail",
        out_shape=(
            jax.ShapeDtypeStruct((1, toks), F32),
            jax.ShapeDtypeStruct((features.shape[1], width), F32),
            jax.ShapeDtypeStruct((classes, width), F32),
        ),
        in_specs=[vmem] * 4,
        out_specs=(vmem,) * 3,
        scratch_shapes=[
            pltpu.VMEM(w.shape, BF16),
            pltpu.VMEM((SIDE, SIDE, toks, width), BF16),
            pltpu.VMEM((2, 2, toks, hcols), BF16),
            pltpu.VMEM((2, SIDE, toks, hcols), BF16),
            pltpu.VMEM((2, 2, toks, hcols), BF16),
            pltpu.VMEM((2, SIDE, toks, hcols), BF16),
            pltpu.VMEM((SIDE, toks, hcols), BF16),
            pltpu.VMEM((SIDE, toks, hcols), BF16),
            pltpu.VMEM((2, tok2, hcols), BF16),
            pltpu.VMEM((2, toks, hcols), BF16),
            pltpu.VMEM((2, tok2, hcols), BF16),
            pltpu.VMEM((2, toks, hcols), BF16),
            pltpu.VMEM((2 * SIDE, classes, classes), F32),
            pltpu.VMEM((classes, toks), F32),
            pltpu.VMEM((classes, toks), F32),
            pltpu.VMEM((SIDE, classes, toks), BF16),
            pltpu.VMEM((SIDE, SIDE, toks, width), BF16),
            pltpu.VMEM((SIDE * SIDE * toks, width), BF16),
            pltpu.VMEM((SIDE, SIDE, classes, toks), BF16),
            pltpu.VMEM((SIDE, SIDE, classes, classes), BF16),
            pltpu.SemaphoreType.DMA((copies,)),
            pltpu.SemaphoreType.DMA((copies,)),
        ],
        compiler_params=pltpu.CompilerParams(
            collective_id=1, has_side_effects=True, vmem_limit_bytes=60 * 1024 * 1024
        ),
    )(w, features, padded, labels.reshape(1, toks))
    return loss.reshape(toks), wgrad, hgrad[: head.shape[0]]


def body(raw_weight, features, head, labels):
    current = raw_weight
    for _ in range(ITERS):
        current = bjorck_step(current)
    row_loss, weight_grad, head_grad = tail(current, features, head, labels)
    return (current, row_loss, weight_grad, head_grad)


def solution(mesh):
    placed = (P("row", "col"), P(None, "row"), P(None, "col"), P("row"))
    return jax.shard_map(
        body,
        mesh=mesh,
        in_specs=placed,
        out_specs=(P("row", "col"), P("row"), P("row", "col"), P(None, "col")),
        check_vma=False,
    )
```

```python
import jax
import jax.numpy as jnp
from jax import lax
from jax.experimental import pallas as pl
from jax.experimental.pallas import tpu as pltpu
from jax.sharding import PartitionSpec as P

CLASSES = 100
ITERS = 2
SIDE = 4
F32 = jnp.float32
BF16 = jnp.bfloat16
MESH = pl.DeviceIdType.MESH
NT = (((1,), (1,)), ((), ()))
TN = (((0,), (0,)), ((), ()))


class Copies:
    def __init__(self, send_sems, recv_sems):
        self.sems = (send_sems, recv_sems)
        self.started = {}

    def send(self, name, src, dst, device):
        index = len(self.started)
        copy = pltpu.make_async_remote_copy(
            src_ref=src, dst_ref=dst, send_sem=self.sems[0].at[index], recv_sem=self.sems[1].at[index],
            device_id=device, device_id_type=MESH,
        )
        copy.start()
        self.started[name] = copy

    def arrived(self, name):
        self.started[name].wait_recv()

    def drain(self):
        for copy in self.started.values():
            copy.wait_send()


def neighbours():
    row, col = lax.axis_index("row"), lax.axis_index("col")
    x, z, y, core = row // SIDE, row % SIDE, col // 2, col % 2
    up = lambda v, d: (v + d) % SIDE
    return dict(
        zp=(x * SIDE + up(z, 1), col), zm=(x * SIDE + up(z, 3), col),
        xp=(up(x, 1) * SIDE + z, col), xm=(up(x, 3) * SIDE + z, col),
        yp=(row, up(y, 1) * 2 + core), ym=(row, up(y, 3) * 2 + core),
        twin=(row, y * 2 + 1 - core),
    )


def greet(devices):
    barrier = pltpu.get_barrier_semaphore()
    for device in devices:
        pl.semaphore_signal(barrier, inc=1, device_id=device, device_id_type=MESH)
    pl.semaphore_wait(barrier, len(devices))


def add_to(ref, *terms):
    total = ref[...].astype(F32)
    for term in terms:
        total = total + term[...].astype(F32)
    ref[...] = total.astype(ref.dtype)


PAIRS = (((1, 1), (0, 1)), ((1, 0), (0, 0)), ((1, 2), (2, 1)), ((2, 2), (1, 3)), ((2, 0), (0, 2)))
WHERE = {offset: (pair, which) for pair, both in enumerate(PAIRS) for which, offset in enumerate(both)}


def bjorck_kernel(
    w_ref, out_ref, az, ax, gp, gr, gh, gf, far, near, px1, px2, px3, pz1, pz2, pfx, pqx, pfz, pqz, zr1, zr2, send_sems, recv_sems
):
    rows, cols = w_ref.shape
    half, quarter, eighth, third = rows // 2, rows // 4, rows // 8, rows // 3
    col = lax.axis_index("col")
    y, core = col // 2, col % 2
    to = neighbours()
    greet(list(to.values()))
    net = Copies(send_sems, recv_sems)

    def block(dy, part=None):
        start = ((y + dy) % SIDE) * quarter
        if part is None:
            return pl.ds(pl.multiple_of(start, quarter), quarter)
        return pl.ds(pl.multiple_of(start + part * eighth, eighth), eighth)

    lo, hi = pl.ds(0, half), pl.ds(half, half)
    top, rest = pl.ds(0, third), pl.ds(third, rows - third)
    az[0] = w_ref[...].astype(BF16)
    own = az.at[0]
    net.send("zm0", own.at[top], az.at[1, top], to["zm"])
    net.send("xm0", own.at[lo], ax.at[1, lo], to["xm"])
    net.send("zp0", own.at[rest], az.at[3, rest], to["zp"])
    net.send("xp0", own.at[hi], ax.at[3, hi], to["xp"])
    net.send("zm1", own.at[rest], az.at[1, rest], to["zm"])
    net.send("xm1", own.at[hi], ax.at[1, hi], to["xm"])
    net.send("xp1", own.at[lo], ax.at[3, lo], to["xp"])
    ax[0] = az[0]
    net.arrived("zm0")
    net.send("zm2", az.at[1, top], az.at[2, top], to["zm"])
    net.arrived("xm0")
    net.send("xm2", ax.at[1, lo], ax.at[2, lo], to["xm"])
    net.arrived("xp0")
    net.send("xp2", ax.at[3, hi], ax.at[2, hi], to["xp"])
    net.arrived("zp0")
    net.send("zp2", az.at[3, rest], az.at[2, rest], to["zp"])
    needs = {0: ("zm1", "xm1"), 1: (), 2: ("xm2", "xp2", "zm2", "zp2"), 3: ("xp1",), 4: ()}

    def partial_gram(p):
        for name in needs[p]:
            net.arrived(name)
        for which, (dz, dx) in enumerate(PAIRS[p]):
            gp[p, which] = lax.dot_general(az[dz], ax[dx], NT, preferred_element_type=F32).astype(BF16)
        net.send(("twin", p), gp.at[p, 1 - core], gr.at[p], to["twin"])

    def chip_sum(p):
        net.arrived(("twin", p))
        gh[p] = (gp[p, core].astype(F32) + gr[p].astype(F32)).astype(BF16)
        net.send(("farp", p), gh.at[p, block(2, 0)], far.at[p, 0], to["yp"])
        net.send(("farm", p), gh.at[p, block(2, 1)], far.at[p, 1], to["ym"])

    def far_sum(p):
        net.arrived(("farp", p))
        add_to(gh.at[p, block(1, 0)], far.at[p, 0])
        net.send(("nearp", p), gh.at[p, block(1)], near.at[p, 0], to["yp"])
        net.arrived(("farm", p))
        add_to(gh.at[p, block(3, 1)], far.at[p, 1])
        net.send(("nearm", p), gh.at[p, block(3)], near.at[p, 1], to["ym"])

    def own_sum(p):
        net.arrived(("nearp", p))
        net.arrived(("nearm", p))
        piece = gf.at[p, core, block(0)]
        piece[...] = (gh[p, block(0)].astype(F32) + near[p, 0].astype(F32) + near[p, 1].astype(F32)).astype(BF16)
        for name in ("yp", "ym", "twin"):
            net.send(("own" + name, p), piece, piece, to[name])

    def pass_on(p):
        net.arrived(("ownym", p))
        piece = gf.at[p, core, block(1, 0)]
        net.send(("passm", p), piece, piece, to["ym"])
        net.arrived(("ownyp", p))
        piece = gf.at[p, core, block(3, 1)]
        net.send(("passp", p), piece, piece, to["yp"])
        for dy in (1, 3):
            piece = gf.at[p, core, block(dy)]
            net.send(("twin%d" % dy, p), piece, piece, to["twin"])

    def pass_far(p):
        net.arrived(("passm", p))
        net.arrived(("passp", p))
        piece = gf.at[p, core, block(2)]
        net.send(("twin2", p), piece, piece, to["twin"])

    def ready(p):
        for name in ("owntwin", "twin1", "twin3", "twin2"):
            net.arrived((name, p))

    def combine(direct, mirrored, put):
        @pl.loop(0, cols // 256)
        def _(n):
            at = pl.ds(pl.multiple_of(n * 256, 256), 256)
            acc = None
            for dz, dx in direct:
                term = jnp.dot(gf[WHERE[dz, dx]], ax[dx, :, at], preferred_element_type=F32)
                acc = term if acc is None else acc + term
            for dz, dx in mirrored:
                term = lax.dot_general(gf[WHERE[dz, dx]], az[dz, :, at], TN, preferred_element_type=F32)
                acc = term if acc is None else acc + term
            put(at, acc)

    def store(ref):
        def put(at, acc):
            ref[:, at] = acc.astype(BF16)
        return put

    def after_two():
        ready(0)
        ready(2)
        combine([], [(1, 2)], store(px2))
        net.send("x2p", px2.at[lo], pfx.at[0], to["xp"])
        net.send("x2m", px2.at[hi], pfx.at[1], to["xm"])
        combine([], [(1, 1), (2, 1), (0, 1)], store(px1))
        net.send("x1h", px1.at[hi], pqx.at[0, hi], to["xp"])

    def after_three():
        ready(1)
        ready(3)
        combine([(2, 1), (2, 2)], [], store(pz2))
        net.send("z2m", pz2.at[rest], zr1, to["zm"])
        net.send("z2p", pz2.at[top], pfz, to["zp"])
        combine([], [(1, 3)], store(px3))
        net.send("x3l", px3.at[lo], pqx.at[1, lo], to["xm"])
        combine([(1, 0), (1, 1), (1, 2), (1, 3)], [], store(pz1))
        net.send("z1r", pz1.at[rest], pqz.at[rest], to["zp"])
        net.arrived("x2p")
        add_to(px1.at[lo], pfx.at[0])
        net.send("x1l", px1.at[lo], pqx.at[0, lo], to["xp"])
        net.arrived("x2m")
        add_to(px3.at[hi], pfx.at[1])
        net.send("x3h", px3.at[hi], pqx.at[1, hi], to["xm"])

    def pass_sums():
        net.arrived("z2m")
        net.send("z2r", zr1, zr2, to["zm"])
        net.arrived("z2p")
        add_to(pz1.at[top], pfz)
        net.send("z1t", pz1.at[top], pqz.at[top], to["zp"])

    def after_four():
        ready(4)

        def put(at, acc):
            out_ref[:, at] = 1.5 * w_ref[:, at] - 0.5 * acc

        combine([(0, 0), (0, 1), (0, 2)], [(1, 0), (2, 0)], put)
        for name in ("x1h", "x3l", "z1r", "x1l", "x3h", "z2r", "z1t"):
            net.arrived(name)
        out_ref[top] -= 0.5 * (pqx[0, top].astype(F32) + pqx[1, top].astype(F32) + pqz[top].astype(F32))
        out_ref[rest] -= 0.5 * (
            pqx[0, rest].astype(F32) + pqx[1, rest].astype(F32) + pqz[rest].astype(F32) + zr2[...].astype(F32)
        )

    def run(*steps):
        for stage, p in steps:
            (partial_gram, chip_sum, far_sum, own_sum, pass_on, pass_far)[stage](p)

    run((0, 0), (0, 1), (1, 0), (1, 1), (2, 0), (2, 1))
    run((0, 2), (3, 0), (0, 3), (3, 1), (1, 2), (1, 3))
    run((4, 0), (2, 2), (4, 1), (2, 3), (0, 4))
    run((5, 0), (3, 2), (5, 1), (1, 4), (3, 3))
    run((4, 2), (2, 4), (4, 3))
    run((5, 2), (3, 4), (5, 3))
    after_two()
    run((4, 4))
    after_three()
    run((5, 4))
    pass_sums()
    after_four()
    net.drain()


def bjorck_step(w):
    rows, cols = w.shape
    vmem = pl.BlockSpec(memory_space=pltpu.VMEM)
    pairs, copies = len(PAIRS), 11 + 13 * len(PAIRS) + 11
    part = lambda *shape: pltpu.VMEM(shape, BF16)
    return pl.pallas_call(
        bjorck_kernel,
        name="bjorck_step",
        out_shape=jax.ShapeDtypeStruct(w.shape, F32),
        in_specs=[vmem],
        out_specs=vmem,
        scratch_shapes=[
            part(SIDE, rows, cols),
            part(SIDE, rows, cols),
            part(pairs, 2, rows, rows),
            part(pairs, rows, rows),
            part(pairs, rows, rows),
            part(pairs, 2, rows, rows),
            part(pairs, 2, rows // 8, rows),
            part(pairs, 2, rows // 4, rows),
            part(rows, cols),
            part(rows, cols),
            part(rows, cols),
            part(rows, cols),
            part(rows, cols),
            part(2, rows // 2, cols),
            part(2, rows, cols),
            part(rows // 3, cols),
            part(rows, cols),
            part(rows - rows // 3, cols),
            part(rows - rows // 3, cols),
            pltpu.SemaphoreType.DMA((copies,)),
            pltpu.SemaphoreType.DMA((copies,)),
        ],
        compiler_params=pltpu.CompilerParams(
            collective_id=0, has_side_effects=True, vmem_limit_bytes=60 * 1024 * 1024
        ),
    )(w)


def gather_ring(net, name, piece, first, second, plus, minus):
    net.send((name, "p"), piece(0), piece(0), plus)
    net.send((name, "m"), piece(0), piece(0), minus)

    def finish():
        net.arrived((name, "m"))
        net.send((name, "fm"), first(1), first(1), minus)
        net.arrived((name, "p"))
        net.send((name, "fp"), second(3), second(3), plus)
        net.arrived((name, "fm"))
        net.arrived((name, "fp"))

    return finish


def tail_kernel(
    w_ref, feat_ref, head_ref, labels_ref, loss_ref, wgrad_ref, hgrad_ref,
    wb, pt, fa, na, fb, nb, sa, sb, f2a, n2a, f2b, n2b, kslots, lself, ltwin, lslots, act, pre, lgq, lgt, send_sems, recv_sems,
):
    row, col = lax.axis_index("row"), lax.axis_index("col")
    x, z, y, core = row // SIDE, row % SIDE, col // 2, col % 2
    toks = labels_ref.shape[1]
    hcols = w_ref.shape[1] // 2
    tok2 = toks // 2
    at = lambda v, d: (v + d) % SIDE
    to = neighbours()
    peers = [(row, at(y, dy) * 2 + (core + dk) % 2) for dy in range(SIDE) for dk in range(2) if (dy, dk) != (0, 0)]
    greet([to["zp"], to["zm"], to["xp"], to["xm"]] + peers)
    net = Copies(send_sems, recv_sems)
    ca, cb = pl.ds(0, hcols), pl.ds(hcols, hcols)
    lo, hi = pl.ds(0, tok2), pl.ds(tok2, tok2)
    classes = head_ref.shape[0]

    kslots[col] = lax.dot_general(head_ref[...], head_ref[...], NT, preferred_element_type=F32)
    for peer, device in enumerate(peers):
        net.send(("k", peer), kslots.at[col], kslots.at[col], device)

    wb[...] = w_ref[...].astype(BF16)
    def forward(dx):
        start = pl.multiple_of(at(x, dx) * SIDE * toks, SIDE * toks)
        part = jnp.dot(feat_ref[pl.ds(start, SIDE * toks), :], wb[...], preferred_element_type=F32)
        pt[dx] = part.astype(BF16).reshape(SIDE, toks, 2 * hcols)

    forward(2)
    net.send("fap", pt.at[2, 0:2, :, ca], fa.at[0], to["xp"])
    net.send("fam", pt.at[2, 2:4, :, ca], fa.at[1], to["xm"])
    forward(1)
    forward(3)
    forward(0)
    net.send("fbp", pt.at[0:2, at(z, 2), :, cb], fb.at[0], to["zp"])
    net.send("fbm", pt.at[2:4, at(z, 2), :, cb], fb.at[1], to["zm"])
    net.arrived("fap")
    add_to(pt.at[1, 0:2, :, ca], fa.at[0])
    net.send("nap", pt.at[1, :, :, ca], na.at[0], to["xp"])
    net.arrived("fam")
    add_to(pt.at[3, 2:4, :, ca], fa.at[1])
    net.send("nam", pt.at[3, :, :, ca], na.at[1], to["xm"])
    net.arrived("fbp")
    add_to(pt.at[0:2, at(z, 1), :, cb], fb.at[0])
    net.send("nbp", pt.at[:, at(z, 1), :, cb], nb.at[0], to["zp"])
    net.arrived("fbm")
    add_to(pt.at[2:4, at(z, 3), :, cb], fb.at[1])
    net.send("nbm", pt.at[:, at(z, 3), :, cb], nb.at[1], to["zm"])

    def sum_a(dz):
        zz = at(z, dz)
        return pt[0, zz, :, ca].astype(F32) + na[0, zz].astype(F32) + na[1, zz].astype(F32)

    def sum_b(dx):
        return pt[dx, z, :, cb].astype(F32) + nb[0, dx].astype(F32) + nb[1, dx].astype(F32)

    net.arrived("nap")
    net.arrived("nam")
    sa[2] = sum_a(2).astype(BF16)
    net.send("f2ap", sa.at[2, lo], f2a.at[0], to["zp"])
    net.send("f2am", sa.at[2, hi], f2a.at[1], to["zm"])
    sa[1] = sum_a(1).astype(BF16)
    sa[3] = sum_a(3).astype(BF16)
    net.arrived("nbp")
    net.arrived("nbm")
    sb[2] = sum_b(2).astype(BF16)
    net.send("f2bp", sb.at[2, lo], f2b.at[0], to["xp"])
    net.send("f2bm", sb.at[2, hi], f2b.at[1], to["xm"])
    sb[1] = sum_b(1).astype(BF16)
    sb[3] = sum_b(3).astype(BF16)
    net.arrived("f2ap")
    add_to(sa.at[1, lo], f2a.at[0])
    net.send("n2ap", sa.at[1], n2a.at[0], to["zp"])
    net.arrived("f2am")
    add_to(sa.at[3, hi], f2a.at[1])
    net.send("n2am", sa.at[3], n2a.at[1], to["zm"])
    net.arrived("f2bp")
    add_to(sb.at[1, lo], f2b.at[0])
    net.send("n2bp", sb.at[1], n2b.at[0], to["xp"])
    net.arrived("f2bm")
    add_to(sb.at[3, hi], f2b.at[1])
    net.send("n2bm", sb.at[3], n2b.at[1], to["xm"])
    own_a, own_b = sum_a(0), sum_b(0)
    net.arrived("n2ap")
    net.arrived("n2am")
    act[x, z, :, ca] = (own_a + n2a[0].astype(F32) + n2a[1].astype(F32)).astype(BF16)
    net.arrived("n2bp")
    net.arrived("n2bm")
    act[x, z, :, cb] = (own_b + n2b[0].astype(F32) + n2b[1].astype(F32)).astype(BF16)

    ga = gather_ring(
        net, "ga", lambda d: act.at[at(x, d), z, :, ca], lambda d: act.at[at(x, d), z, lo, ca],
        lambda d: act.at[at(x, d), z, hi, ca], to["xp"], to["xm"],
    )
    gb = gather_ring(
        net, "gb", lambda d: act.at[x, at(z, d), :, cb], lambda d: act.at[x, at(z, d), lo, cb],
        lambda d: act.at[x, at(z, d), hi, cb], to["zp"], to["zm"],
    )
    own_act = jnp.tanh(act[x, z].astype(F32)).astype(BF16)
    lself[...] = lax.dot_general(head_ref[...], own_act, NT, preferred_element_type=F32)
    net.send("ltwin", lself, ltwin, to["twin"])
    ga()
    g2a = gather_ring(
        net, "g2a", lambda d: act.at[:, at(z, d), :, ca], lambda d: act.at[0:2, at(z, d), :, ca],
        lambda d: act.at[2:4, at(z, d), :, ca], to["zp"], to["zm"],
    )
    gb()
    g2b = gather_ring(
        net, "g2b", lambda d: act.at[at(x, d), :, :, cb], lambda d: act.at[at(x, d), 0:2, :, cb],
        lambda d: act.at[at(x, d), 2:4, :, cb], to["xp"], to["xm"],
    )
    net.arrived("ltwin")
    lslots[y] = (lself[...] + ltwin[...]).astype(BF16)
    for dy in (1, 2, 3):
        net.send(("l", dy), lslots.at[y], lslots.at[y], (row, at(y, dy) * 2 + core))

    for peer in range(len(peers)):
        net.arrived(("k", peer))
    pair_products = kslots[0]
    for other in range(1, 2 * SIDE):
        pair_products = pair_products + kslots[other]
    ids = lax.broadcasted_iota(jnp.int32, (classes, classes), 0)
    eye = ids == lax.broadcasted_iota(jnp.int32, (classes, classes), 1)
    class_ids = lax.broadcasted_iota(jnp.int32, (classes, toks), 0)
    one_hot = (class_ids == labels_ref[...]).astype(F32)
    high = lax.Precision.HIGHEST
    norms = jnp.sum(jnp.where(eye, pair_products, 0.0), axis=1, keepdims=True)
    inner = jnp.dot(pair_products, one_hot, precision=high, preferred_element_type=F32)
    own_norm = jnp.sum(one_hot * norms, axis=0, keepdims=True)
    distance = own_norm + norms - 2.0 * inner + 1e-05
    lipschitz = jnp.sqrt(jnp.where(one_hot > 0, 1.0, distance))

    for dy in (1, 2, 3):
        net.arrived(("l", dy))
    logits = lslots[0].astype(F32)
    for other in range(1, SIDE):
        logits = logits + lslots[other].astype(F32)
    real = (class_ids < CLASSES).astype(F32)
    plain_exp = real * jnp.exp(logits)
    bound_exp = (real - one_hot) * jnp.exp(logits + lipschitz)
    partition = jnp.sum(plain_exp, axis=0, keepdims=True) + jnp.sum(bound_exp, axis=0, keepdims=True)
    loss_ref[...] = jnp.log(partition) - jnp.sum(one_hot * logits, axis=0, keepdims=True)
    logit_grad = (plain_exp + bound_exp) / partition - one_hot
    dist_grad = bound_exp / (partition * 2.0 * lipschitz)
    lgq[x, z] = logit_grad.astype(BF16)
    pairs = lax.dot_general(one_hot, dist_grad, NT, precision=high, preferred_element_type=F32)
    pairs = pairs + lax.dot_general(dist_grad, one_hot, NT, precision=high, preferred_element_type=F32)
    lgt[x, z] = pairs.astype(BF16)
    cl, ch = pl.ds(0, classes // 2), pl.ds(classes // 2, classes // 2)
    gl = gather_ring(
        net, "gl", lambda d: lgq.at[at(x, d), z], lambda d: lgq.at[at(x, d), z, cl],
        lambda d: lgq.at[at(x, d), z, ch], to["xp"], to["xm"],
    )
    gt = gather_ring(
        net, "gt", lambda d: lgt.at[x, at(z, d)], lambda d: lgt.at[x, at(z, d), cl],
        lambda d: lgt.at[x, at(z, d), ch], to["zp"], to["zm"],
    )
    gl()
    g2l = gather_ring(
        net, "g2l", lambda d: lgq.at[:, at(z, d)], lambda d: lgq.at[0:2, at(z, d)],
        lambda d: lgq.at[2:4, at(z, d)], to["zp"], to["zm"],
    )
    gt()
    g2t = gather_ring(
        net, "g2t", lambda d: lgt.at[at(x, d)], lambda d: lgt.at[at(x, d), 0:2],
        lambda d: lgt.at[at(x, d), 2:4], to["xp"], to["xm"],
    )
    g2a()
    g2b()
    g2l()
    g2t()

    total = jnp.zeros((classes, classes), F32)
    for block in range(SIDE * SIDE):
        total = total + lgt[block // SIDE, block % SIDE].astype(F32)
    laplace = jnp.where(eye, jnp.sum(total, axis=1, keepdims=True), 0.0) - total
    hgrad_ref[...] = 2.0 * jnp.dot(laplace, head_ref[...].astype(F32), precision=high, preferred_element_type=F32)

    @pl.loop(0, SIDE * SIDE)
    def _(block):
        bx, bz = block // SIDE, block % SIDE
        tokens = pl.ds(pl.multiple_of(block * toks, toks), toks)
        grads = lgq[bx, bz]
        active = jnp.tanh(act[bx, bz].astype(F32))
        act_grad = lax.dot_general(grads, head_ref[...], TN, preferred_element_type=F32)
        pre_grad = (act_grad * (1.0 - active * active)).astype(BF16)
        pre[tokens, :] = pre_grad
        hgrad_ref[...] += jnp.dot(grads, active.astype(BF16), preferred_element_type=F32)

    @pl.loop(0, 3)
    def _(n):
        cols = pl.ds(pl.multiple_of(n * 256, 256), 256)
        wgrad_ref[:, cols] = lax.dot_general(feat_ref[...], pre[:, cols], TN, preferred_element_type=F32)

    net.drain()


def tail(w, features, head, labels):
    toks, width = labels.shape[0], head.shape[1]
    hcols, tok2 = width // 2, toks // 2
    classes = 128
    padded = jnp.pad(head, ((0, classes - head.shape[0]), (0, 0)))
    vmem = pl.BlockSpec(memory_space=pltpu.VMEM)
    copies = 7 + 16 + 4 * 8 + 1 + 3
    loss, wgrad, hgrad = pl.pallas_call(
        tail_kernel,
        name="tail",
        out_shape=(
            jax.ShapeDtypeStruct((1, toks), F32),
            jax.ShapeDtypeStruct((features.shape[1], width), F32),
            jax.ShapeDtypeStruct((classes, width), F32),
        ),
        in_specs=[vmem] * 4,
        out_specs=(vmem,) * 3,
        scratch_shapes=[
            pltpu.VMEM(w.shape, BF16),
            pltpu.VMEM((SIDE, SIDE, toks, width), BF16),
            pltpu.VMEM((2, 2, toks, hcols), BF16),
            pltpu.VMEM((2, SIDE, toks, hcols), BF16),
            pltpu.VMEM((2, 2, toks, hcols), BF16),
            pltpu.VMEM((2, SIDE, toks, hcols), BF16),
            pltpu.VMEM((SIDE, toks, hcols), BF16),
            pltpu.VMEM((SIDE, toks, hcols), BF16),
            pltpu.VMEM((2, tok2, hcols), BF16),
            pltpu.VMEM((2, toks, hcols), BF16),
            pltpu.VMEM((2, tok2, hcols), BF16),
            pltpu.VMEM((2, toks, hcols), BF16),
            pltpu.VMEM((2 * SIDE, classes, classes), F32),
            pltpu.VMEM((classes, toks), F32),
            pltpu.VMEM((classes, toks), F32),
            pltpu.VMEM((SIDE, classes, toks), BF16),
            pltpu.VMEM((SIDE, SIDE, toks, width), BF16),
            pltpu.VMEM((SIDE * SIDE * toks, width), BF16),
            pltpu.VMEM((SIDE, SIDE, classes, toks), BF16),
            pltpu.VMEM((SIDE, SIDE, classes, classes), BF16),
            pltpu.SemaphoreType.DMA((copies,)),
            pltpu.SemaphoreType.DMA((copies,)),
        ],
        compiler_params=pltpu.CompilerParams(
            collective_id=1, has_side_effects=True, vmem_limit_bytes=60 * 1024 * 1024
        ),
    )(w, features, padded, labels.reshape(1, toks))
    return loss.reshape(toks), wgrad, hgrad[: head.shape[0]]


def body(raw_weight, features, head, labels):
    current = raw_weight
    for _ in range(ITERS):
        current = bjorck_step(current)
    row_loss, weight_grad, head_grad = tail(current, features, head, labels)
    return (current, row_loss, weight_grad, head_grad)


def solution(mesh):
    placed = (P("row", "col"), P(None, "row"), P(None, "col"), P("row"))
    return jax.shard_map(
        body,
        mesh=mesh,
        in_specs=placed,
        out_specs=(P("row", "col"), P("row"), P("row", "col"), P(None, "col")),
        check_vma=False,
    )
```

```python
import jax
import jax.numpy as jnp
from jax import lax
from jax.experimental import pallas as pl
from jax.experimental.pallas import tpu as pltpu
from jax.sharding import PartitionSpec as P

CLASSES = 100
ITERS = 2
SIDE = 4
F32 = jnp.float32
BF16 = jnp.bfloat16
MESH = pl.DeviceIdType.MESH
NT = (((1,), (1,)), ((), ()))
TN = (((0,), (0,)), ((), ()))


class Copies:
    def __init__(self, send_sems, recv_sems):
        self.sems = (send_sems, recv_sems)
        self.started = {}

    def send(self, name, src, dst, device):
        index = len(self.started)
        copy = pltpu.make_async_remote_copy(
            src_ref=src, dst_ref=dst, send_sem=self.sems[0].at[index], recv_sem=self.sems[1].at[index],
            device_id=device, device_id_type=MESH,
        )
        copy.start()
        self.started[name] = copy

    def arrived(self, name):
        self.started[name].wait_recv()

    def drain(self):
        for copy in self.started.values():
            copy.wait_send()


def neighbours():
    row, col = lax.axis_index("row"), lax.axis_index("col")
    x, z, y, core = row // SIDE, row % SIDE, col // 2, col % 2
    up = lambda v, d: (v + d) % SIDE
    return dict(
        zp=(x * SIDE + up(z, 1), col), zm=(x * SIDE + up(z, 3), col),
        xp=(up(x, 1) * SIDE + z, col), xm=(up(x, 3) * SIDE + z, col),
        yp=(row, up(y, 1) * 2 + core), ym=(row, up(y, 3) * 2 + core),
        twin=(row, y * 2 + 1 - core),
    )


def greet(devices):
    barrier = pltpu.get_barrier_semaphore()
    for device in devices:
        pl.semaphore_signal(barrier, inc=1, device_id=device, device_id_type=MESH)
    pl.semaphore_wait(barrier, len(devices))


def add_to(ref, *terms):
    total = ref[...].astype(F32)
    for term in terms:
        total = total + term[...].astype(F32)
    ref[...] = total.astype(ref.dtype)


PAIRS = (((1, 1), (0, 1)), ((1, 0), (0, 0)), ((1, 2), (2, 1)), ((2, 2), (1, 3)), ((2, 0), (0, 2)))
WHERE = {offset: (pair, which) for pair, both in enumerate(PAIRS) for which, offset in enumerate(both)}


def bjorck_kernel(
    w_ref, out_ref, az, ax, gp, gr, gh, gf, far, near, px1, px2, px3, pz1, pz2, pfx, pqx, pfz, pqz, zr1, zr2, send_sems, recv_sems
):
    rows, cols = w_ref.shape
    half, quarter, eighth, third = rows // 2, rows // 4, rows // 8, rows // 3
    col = lax.axis_index("col")
    y, core = col // 2, col % 2
    to = neighbours()
    greet(list(to.values()))
    net = Copies(send_sems, recv_sems)

    def block(dy, part=None):
        start = ((y + dy) % SIDE) * quarter
        if part is None:
            return pl.ds(pl.multiple_of(start, quarter), quarter)
        return pl.ds(pl.multiple_of(start + part * eighth, eighth), eighth)

    lo, hi = pl.ds(0, half), pl.ds(half, half)
    top, rest = pl.ds(0, third), pl.ds(third, rows - third)
    az[0] = w_ref[...].astype(BF16)
    own = az.at[0]
    net.send("zm0", own.at[top], az.at[1, top], to["zm"])
    net.send("xm0", own.at[lo], ax.at[1, lo], to["xm"])
    net.send("zp0", own.at[rest], az.at[3, rest], to["zp"])
    net.send("xp0", own.at[hi], ax.at[3, hi], to["xp"])
    net.send("zm1", own.at[rest], az.at[1, rest], to["zm"])
    net.send("xm1", own.at[hi], ax.at[1, hi], to["xm"])
    net.send("xp1", own.at[lo], ax.at[3, lo], to["xp"])
    ax[0] = az[0]
    net.arrived("zm0")
    net.send("zm2", az.at[1, top], az.at[2, top], to["zm"])
    net.arrived("xm0")
    net.send("xm2", ax.at[1, lo], ax.at[2, lo], to["xm"])
    net.arrived("xp0")
    net.send("xp2", ax.at[3, hi], ax.at[2, hi], to["xp"])
    net.arrived("zp0")
    net.send("zp2", az.at[3, rest], az.at[2, rest], to["zp"])
    needs = {0: ("zm1", "xm1"), 1: (), 2: ("xm2", "xp2", "zm2", "zp2"), 3: ("xp1",), 4: ()}

    def partial_gram(p):
        for name in needs[p]:
            net.arrived(name)
        for which, (dz, dx) in enumerate(PAIRS[p]):
            gp[p, which] = lax.dot_general(az[dz], ax[dx], NT, preferred_element_type=F32).astype(BF16)
        net.send(("twin", p), gp.at[p, 1 - core], gr.at[p], to["twin"])

    def chip_sum(p):
        net.arrived(("twin", p))
        gh[p] = (gp[p, core].astype(F32) + gr[p].astype(F32)).astype(BF16)
        net.send(("farp", p), gh.at[p, block(2, 0)], far.at[p, 0], to["yp"])
        net.send(("farm", p), gh.at[p, block(2, 1)], far.at[p, 1], to["ym"])

    def far_sum(p):
        net.arrived(("farp", p))
        add_to(gh.at[p, block(1, 0)], far.at[p, 0])
        net.send(("nearp", p), gh.at[p, block(1)], near.at[p, 0], to["yp"])
        net.arrived(("farm", p))
        add_to(gh.at[p, block(3, 1)], far.at[p, 1])
        net.send(("nearm", p), gh.at[p, block(3)], near.at[p, 1], to["ym"])

    def own_sum(p):
        net.arrived(("nearp", p))
        net.arrived(("nearm", p))
        piece = gf.at[p, core, block(0)]
        piece[...] = (gh[p, block(0)].astype(F32) + near[p, 0].astype(F32) + near[p, 1].astype(F32)).astype(BF16)
        for name in ("yp", "ym", "twin"):
            net.send(("own" + name, p), piece, piece, to[name])

    def pass_on(p):
        net.arrived(("ownym", p))
        piece = gf.at[p, core, block(1, 0)]
        net.send(("passm", p), piece, piece, to["ym"])
        net.arrived(("ownyp", p))
        piece = gf.at[p, core, block(3, 1)]
        net.send(("passp", p), piece, piece, to["yp"])
        for dy in (1, 3):
            piece = gf.at[p, core, block(dy)]
            net.send(("twin%d" % dy, p), piece, piece, to["twin"])

    def pass_far(p):
        net.arrived(("passm", p))
        net.arrived(("passp", p))
        piece = gf.at[p, core, block(2)]
        net.send(("twin2", p), piece, piece, to["twin"])

    def ready(p):
        for name in ("owntwin", "twin1", "twin3", "twin2"):
            net.arrived((name, p))

    def combine(direct, mirrored, put):
        @pl.loop(0, cols // 256)
        def _(n):
            at = pl.ds(pl.multiple_of(n * 256, 256), 256)
            acc = None
            for dz, dx in direct:
                term = jnp.dot(gf[WHERE[dz, dx]], ax[dx, :, at], preferred_element_type=F32)
                acc = term if acc is None else acc + term
            for dz, dx in mirrored:
                term = lax.dot_general(gf[WHERE[dz, dx]], az[dz, :, at], TN, preferred_element_type=F32)
                acc = term if acc is None else acc + term
            put(at, acc)

    def store(ref):
        def put(at, acc):
            ref[:, at] = acc.astype(BF16)
        return put

    def after_two():
        ready(0)
        ready(2)
        combine([], [(1, 2)], store(px2))
        net.send("x2p", px2.at[lo], pfx.at[0], to["xp"])
        net.send("x2m", px2.at[hi], pfx.at[1], to["xm"])
        combine([], [(1, 1), (2, 1), (0, 1)], store(px1))
        net.send("x1h", px1.at[hi], pqx.at[0, hi], to["xp"])

    def after_three():
        ready(1)
        ready(3)
        combine([(2, 1), (2, 2)], [], store(pz2))
        net.send("z2m", pz2.at[rest], zr1, to["zm"])
        net.send("z2p", pz2.at[top], pfz, to["zp"])
        combine([], [(1, 3)], store(px3))
        net.send("x3l", px3.at[lo], pqx.at[1, lo], to["xm"])
        combine([(1, 0), (1, 1), (1, 2), (1, 3)], [], store(pz1))
        net.send("z1r", pz1.at[rest], pqz.at[rest], to["zp"])
        net.arrived("x2p")
        add_to(px1.at[lo], pfx.at[0])
        net.send("x1l", px1.at[lo], pqx.at[0, lo], to["xp"])
        net.arrived("x2m")
        add_to(px3.at[hi], pfx.at[1])
        net.send("x3h", px3.at[hi], pqx.at[1, hi], to["xm"])

    def pass_sums():
        net.arrived("z2m")
        net.send("z2r", zr1, zr2, to["zm"])
        net.arrived("z2p")
        add_to(pz1.at[top], pfz)
        net.send("z1t", pz1.at[top], pqz.at[top], to["zp"])

    def after_four():
        ready(4)

        def put(at, acc):
            out_ref[:, at] = 1.5 * w_ref[:, at] - 0.5 * acc

        combine([(0, 0), (0, 1), (0, 2)], [(1, 0), (2, 0)], put)
        for name in ("x1h", "x3l", "z1r", "x1l", "x3h", "z2r", "z1t"):
            net.arrived(name)
        out_ref[top] -= 0.5 * (pqx[0, top].astype(F32) + pqx[1, top].astype(F32) + pqz[top].astype(F32))
        out_ref[rest] -= 0.5 * (
            pqx[0, rest].astype(F32) + pqx[1, rest].astype(F32) + pqz[rest].astype(F32) + zr2[...].astype(F32)
        )

    def run(*steps):
        for stage, p in steps:
            (partial_gram, chip_sum, far_sum, own_sum, pass_on, pass_far)[stage](p)

    run((0, 0), (0, 1), (1, 0), (1, 1), (2, 0), (2, 1))
    run((0, 2), (3, 0), (0, 3), (3, 1), (1, 2), (1, 3))
    run((4, 0), (2, 2), (4, 1), (2, 3), (0, 4))
    run((5, 0), (3, 2), (5, 1), (1, 4), (3, 3))
    run((4, 2), (2, 4), (4, 3))
    run((5, 2), (3, 4), (5, 3))
    after_two()
    run((4, 4))
    after_three()
    run((5, 4))
    pass_sums()
    after_four()
    net.drain()


def bjorck_step(w):
    rows, cols = w.shape
    vmem = pl.BlockSpec(memory_space=pltpu.VMEM)
    pairs, copies = len(PAIRS), 11 + 13 * len(PAIRS) + 11
    part = lambda *shape: pltpu.VMEM(shape, BF16)
    return pl.pallas_call(
        bjorck_kernel,
        name="bjorck_step",
        out_shape=jax.ShapeDtypeStruct(w.shape, F32),
        in_specs=[vmem],
        out_specs=vmem,
        scratch_shapes=[
            part(SIDE, rows, cols),
            part(SIDE, rows, cols),
            part(pairs, 2, rows, rows),
            part(pairs, rows, rows),
            part(pairs, rows, rows),
            part(pairs, 2, rows, rows),
            part(pairs, 2, rows // 8, rows),
            part(pairs, 2, rows // 4, rows),
            part(rows, cols),
            part(rows, cols),
            part(rows, cols),
            part(rows, cols),
            part(rows, cols),
            part(2, rows // 2, cols),
            part(2, rows, cols),
            part(rows // 3, cols),
            part(rows, cols),
            part(rows - rows // 3, cols),
            part(rows - rows // 3, cols),
            pltpu.SemaphoreType.DMA((copies,)),
            pltpu.SemaphoreType.DMA((copies,)),
        ],
        compiler_params=pltpu.CompilerParams(
            collective_id=0, has_side_effects=True, vmem_limit_bytes=60 * 1024 * 1024
        ),
    )(w)


def gather_ring(net, name, piece, first, second, plus, minus):
    net.send((name, "p"), piece(0), piece(0), plus)
    net.send((name, "m"), piece(0), piece(0), minus)

    def forward():
        net.arrived((name, "m"))
        net.send((name, "fm"), first(1), first(1), minus)
        net.arrived((name, "p"))
        net.send((name, "fp"), second(3), second(3), plus)

    def wait():
        net.arrived((name, "fm"))
        net.arrived((name, "fp"))

    return forward, wait


def tail_kernel(
    w_ref, feat_ref, given_head_ref, labels_ref, loss_ref, wgrad_ref, hgrad_ref,
    head_ref, wb, pt, fa, na, fb, nb, sa, sb, f2a, n2a, f2b, n2b, kslots, lself, ltwin, lslots, act, active, slope, pre, lfull, lgq, grads,
    send_sems, recv_sems,
):
    row, col = lax.axis_index("row"), lax.axis_index("col")
    x, z, y, core = row // SIDE, row % SIDE, col // 2, col % 2
    toks = labels_ref.shape[1]
    width = w_ref.shape[1]
    hcols = width // 2
    tok2 = toks // 2
    at = lambda v, d: (v + d) % SIDE
    to = neighbours()
    peers = [(row, at(y, dy) * 2 + (core + dk) % 2) for dy in range(SIDE) for dk in range(2) if (dy, dk) != (0, 0)]
    steps = sorted(((dx, dz) for dx in range(SIDE) for dz in range(SIDE) if (dx, dz) != (0, 0)), key=lambda d: -(d[0] == 2) - (d[1] == 2))
    plane = [(at(x, dx) * SIDE + at(z, dz), col) for dx, dz in steps]
    greet(plane + peers)
    net = Copies(send_sems, recv_sems)
    ca, cb = pl.ds(0, hcols), pl.ds(hcols, hcols)
    lo, hi = pl.ds(0, tok2), pl.ds(tok2, tok2)
    classes = head_ref.shape[0]
    wb[...] = w_ref[...].astype(BF16)

    def forward(dx):
        start = pl.multiple_of(at(x, dx) * SIDE * toks, SIDE * toks)
        part = jnp.dot(feat_ref[pl.ds(start, SIDE * toks), :], wb[...], preferred_element_type=F32)
        pt[dx] = part.astype(BF16).reshape(SIDE, toks, width)

    forward(2)
    net.send("fap", pt.at[2, 0:2, :, ca], fa.at[0], to["xp"])
    net.send("fam", pt.at[2, 2:4, :, ca], fa.at[1], to["xm"])
    forward(1)
    net.send("nap1", pt.at[1, 2:4, :, ca], na.at[0, 2:4], to["xp"])
    forward(3)
    net.send("nam1", pt.at[3, 0:2, :, ca], na.at[1, 0:2], to["xm"])
    forward(0)
    net.send("fbp", pt.at[0:2, at(z, 2), :, cb], fb.at[0], to["zp"])
    net.send("fbm", pt.at[2:4, at(z, 2), :, cb], fb.at[1], to["zm"])
    net.send("nbp1", pt.at[2:4, at(z, 1), :, cb], nb.at[0, 2:4], to["zp"])
    net.send("nbm1", pt.at[0:2, at(z, 3), :, cb], nb.at[1, 0:2], to["zm"])
    net.arrived("fap")
    add_to(pt.at[1, 0:2, :, ca], fa.at[0])
    net.send("nap2", pt.at[1, 0:2, :, ca], na.at[0, 0:2], to["xp"])
    net.arrived("fam")
    add_to(pt.at[3, 2:4, :, ca], fa.at[1])
    net.send("nam2", pt.at[3, 2:4, :, ca], na.at[1, 2:4], to["xm"])

    real_classes = given_head_ref.shape[0]
    head_ref[...] = jnp.zeros_like(head_ref)
    head_ref[0:real_classes, :] = given_head_ref[...]
    kslots[col] = lax.dot_general(head_ref[...], head_ref[...], NT, preferred_element_type=F32)
    for peer, device in enumerate(peers):
        net.send(("k", peer), kslots.at[col], kslots.at[col], device)

    net.arrived("fbp")
    add_to(pt.at[0:2, at(z, 1), :, cb], fb.at[0])
    net.send("nbp2", pt.at[0:2, at(z, 1), :, cb], nb.at[0, 0:2], to["zp"])
    net.arrived("fbm")
    add_to(pt.at[2:4, at(z, 3), :, cb], fb.at[1])
    net.send("nbm2", pt.at[2:4, at(z, 3), :, cb], nb.at[1, 2:4], to["zm"])

    def sum_a(dz):
        zz = at(z, dz)
        return pt[0, zz, :, ca].astype(F32) + na[0, zz].astype(F32) + na[1, zz].astype(F32)

    def sum_b(dx):
        return pt[dx, z, :, cb].astype(F32) + nb[0, dx].astype(F32) + nb[1, dx].astype(F32)

    for name in ("nap1", "nam1", "nap2", "nam2"):
        net.arrived(name)
    sa[2] = sum_a(2).astype(BF16)
    net.send("f2ap", sa.at[2, lo], f2a.at[0], to["zp"])
    net.send("f2am", sa.at[2, hi], f2a.at[1], to["zm"])
    sa[1] = sum_a(1).astype(BF16)
    net.send("n2ap1", sa.at[1, hi], n2a.at[0, hi], to["zp"])
    sa[3] = sum_a(3).astype(BF16)
    net.send("n2am1", sa.at[3, lo], n2a.at[1, lo], to["zm"])
    for name in ("nbp1", "nbm1", "nbp2", "nbm2"):
        net.arrived(name)
    sb[2] = sum_b(2).astype(BF16)
    net.send("f2bp", sb.at[2, lo], f2b.at[0], to["xp"])
    net.send("f2bm", sb.at[2, hi], f2b.at[1], to["xm"])
    sb[1] = sum_b(1).astype(BF16)
    net.send("n2bp1", sb.at[1, hi], n2b.at[0, hi], to["xp"])
    sb[3] = sum_b(3).astype(BF16)
    net.send("n2bm1", sb.at[3, lo], n2b.at[1, lo], to["xm"])
    net.arrived("f2ap")
    add_to(sa.at[1, lo], f2a.at[0])
    net.send("n2ap2", sa.at[1, lo], n2a.at[0, lo], to["zp"])
    net.arrived("f2am")
    add_to(sa.at[3, hi], f2a.at[1])
    net.send("n2am2", sa.at[3, hi], n2a.at[1, hi], to["zm"])
    net.arrived("f2bp")
    add_to(sb.at[1, lo], f2b.at[0])
    net.send("n2bp2", sb.at[1, lo], n2b.at[0, lo], to["xp"])
    net.arrived("f2bm")
    add_to(sb.at[3, hi], f2b.at[1])
    net.send("n2bm2", sb.at[3, hi], n2b.at[1, hi], to["xm"])
    own_a, own_b = sum_a(0), sum_b(0)

    for name in ("n2ap1", "n2am1", "n2ap2", "n2am2"):
        net.arrived(name)
    act[x, z, :, ca] = (own_a + n2a[0].astype(F32) + n2a[1].astype(F32)).astype(BF16)
    ga_forward, ga_wait = gather_ring(
        net, "ga", lambda d: act.at[at(x, d), z, :, ca], lambda d: act.at[at(x, d), z, lo, ca],
        lambda d: act.at[at(x, d), z, hi, ca], to["xp"], to["xm"],
    )
    for name in ("n2bp1", "n2bm1", "n2bp2", "n2bm2"):
        net.arrived(name)
    act[x, z, :, cb] = (own_b + n2b[0].astype(F32) + n2b[1].astype(F32)).astype(BF16)
    gb_forward, gb_wait = gather_ring(
        net, "gb", lambda d: act.at[x, at(z, d), :, cb], lambda d: act.at[x, at(z, d), lo, cb],
        lambda d: act.at[x, at(z, d), hi, cb], to["zp"], to["zm"],
    )
    own_act = jnp.tanh(act[x, z].astype(F32)).astype(BF16)
    lself[...] = lax.dot_general(head_ref[...], own_act, NT, preferred_element_type=F32)
    net.send("ltwin", lself, ltwin, to["twin"])

    for peer in range(len(peers)):
        net.arrived(("k", peer))
    pair_products = kslots[0]
    for other in range(1, 2 * SIDE):
        pair_products = pair_products + kslots[other]
    ids = lax.broadcasted_iota(jnp.int32, (classes, classes), 0)
    eye = ids == lax.broadcasted_iota(jnp.int32, (classes, classes), 1)
    class_ids = lax.broadcasted_iota(jnp.int32, (classes, toks), 0)
    one_hot = (class_ids == labels_ref[...]).astype(F32)
    high = lax.Precision.HIGHEST
    norms = jnp.sum(jnp.where(eye, pair_products, 0.0), axis=1, keepdims=True)
    inner = jnp.dot(pair_products, one_hot, precision=high, preferred_element_type=F32)
    own_norm = jnp.sum(one_hot * norms, axis=0, keepdims=True)
    distance = own_norm + norms - 2.0 * inner + 1e-05
    lipschitz = jnp.sqrt(jnp.where(one_hot > 0, 1.0, distance))

    net.arrived("ltwin")
    lslots[y] = (lself[...] + ltwin[...]).astype(BF16)
    for dy in (1, 2, 3):
        net.send(("l", dy), lslots.at[y], lslots.at[y], (row, at(y, dy) * 2 + core))
    ga_forward()
    gb_forward()
    for dy in (1, 2, 3):
        net.arrived(("l", dy))
    logits = lslots[0].astype(F32)
    for other in range(1, SIDE):
        logits = logits + lslots[other].astype(F32)
    real = (class_ids < CLASSES).astype(F32)
    plain_exp = real * jnp.exp(logits)
    bound_exp = (real - one_hot) * jnp.exp(logits + lipschitz)
    partition = jnp.sum(plain_exp, axis=0, keepdims=True) + jnp.sum(bound_exp, axis=0, keepdims=True)
    loss_ref[...] = jnp.log(partition) - jnp.sum(one_hot * logits, axis=0, keepdims=True)
    logit_grad = (plain_exp + bound_exp) / partition - one_hot
    dist_grad = bound_exp / (partition * 2.0 * lipschitz)
    pairs = lax.dot_general(one_hot, dist_grad, NT, precision=high, preferred_element_type=F32)
    pairs = pairs + lax.dot_general(dist_grad, one_hot, NT, precision=high, preferred_element_type=F32)
    for which, term in enumerate((logit_grad, pairs)):
        lfull[0, which] = term[0 : classes // 2].astype(BF16)
        lfull[1, which] = term[classes // 2 :].astype(BF16)
    lgq[x, z, core] = lfull[core]
    for peer, device in enumerate(plane):
        net.send(("g", peer), lgq.at[x, z, core], lgq.at[x, z, core], device)

    ga_wait()
    g2a_forward, g2a_wait = gather_ring(
        net, "g2a", lambda d: act.at[:, at(z, d), :, ca], lambda d: act.at[0:2, at(z, d), :, ca],
        lambda d: act.at[2:4, at(z, d), :, ca], to["zp"], to["zm"],
    )
    gb_wait()
    g2b_forward, g2b_wait = gather_ring(
        net, "g2b", lambda d: act.at[at(x, d), :, :, cb], lambda d: act.at[at(x, d), 0:2, :, cb],
        lambda d: act.at[at(x, d), 2:4, :, cb], to["xp"], to["xm"],
    )

    def activate(bx, bz, cols):
        tokens = pl.ds(pl.multiple_of((bx * SIDE + bz) * toks, toks), toks)
        value = jnp.tanh(act[bx, bz, :, cols].astype(F32))
        active[tokens, cols] = value.astype(BF16)
        slope[tokens, cols] = 1.0 - value * value

    def activate_both(d):
        @pl.loop(0, SIDE)
        def _(i):
            activate(i, at(z, d), ca)
            activate(at(x, d), i, cb)

    activate_both(0)
    for peer in range(len(plane)):
        net.arrived(("g", peer))
    net.send("gtwin", lgq.at[:, :, core], lgq.at[:, :, core], to["twin"])
    g2a_forward()
    g2b_forward()
    activate_both(1)
    activate_both(3)
    net.arrived("gtwin")
    total = jnp.zeros((classes, classes), F32)
    for block in range(SIDE * SIDE):
        bx, bz = block // SIDE, block % SIDE
        grads[:, block * toks : (block + 1) * toks] = lgq[bx, bz, :, 0].reshape(classes, toks)
        total = total + lgq[bx, bz, :, 1].reshape(classes, classes).astype(F32)
    laplace = jnp.where(eye, jnp.sum(total, axis=1, keepdims=True), 0.0) - total
    spread = 2.0 * jnp.dot(laplace, head_ref[...].astype(F32), precision=high, preferred_element_type=F32)
    hgrad_ref[...] = spread[0:real_classes]
    g2a_wait()
    g2b_wait()
    activate_both(2)

    @pl.loop(0, SIDE)
    def _(block):
        tokens = pl.ds(pl.multiple_of(block * SIDE * toks, SIDE * toks), SIDE * toks)
        act_grad = lax.dot_general(grads[:, tokens], head_ref[...], TN, preferred_element_type=F32)
        pre[tokens, :] = (act_grad * slope[tokens, :]).astype(BF16)

    @pl.loop(0, width // 256)
    def _(n):
        cols = pl.ds(pl.multiple_of(n * 256, 256), 256)
        wgrad_ref[:, cols] = lax.dot_general(feat_ref[...], pre[:, cols], TN, preferred_element_type=F32)
        hgrad_ref[:, cols] += jnp.dot(grads[...], active[:, cols], preferred_element_type=F32)[0:real_classes]

    net.drain()


def tail(w, features, head, labels):
    toks, width = labels.shape[0], head.shape[1]
    hcols, tok2, rows = width // 2, toks // 2, SIDE * SIDE
    classes = 128
    vmem = pl.BlockSpec(memory_space=pltpu.VMEM)
    copies = 7 + 12 + 12 + 16 + 1 + 3 + 15 + 1
    part = lambda *shape: pltpu.VMEM(shape, BF16)
    loss, wgrad, hgrad = pl.pallas_call(
        tail_kernel,
        name="tail",
        out_shape=(
            jax.ShapeDtypeStruct((1, toks), F32),
            jax.ShapeDtypeStruct(w.shape, F32),
            jax.ShapeDtypeStruct(head.shape, F32),
        ),
        in_specs=[vmem] * 4,
        out_specs=(vmem,) * 3,
        scratch_shapes=[
            part(classes, width),
            part(*w.shape),
            part(SIDE, SIDE, toks, width),
            part(2, 2, toks, hcols),
            part(2, SIDE, toks, hcols),
            part(2, 2, toks, hcols),
            part(2, SIDE, toks, hcols),
            part(SIDE, toks, hcols),
            part(SIDE, toks, hcols),
            part(2, tok2, hcols),
            part(2, toks, hcols),
            part(2, tok2, hcols),
            part(2, toks, hcols),
            pltpu.VMEM((2 * SIDE, classes, classes), F32),
            pltpu.VMEM((classes, toks), F32),
            pltpu.VMEM((classes, toks), F32),
            part(SIDE, classes, toks),
            part(SIDE, SIDE, toks, width),
            part(rows * toks, width),
            pltpu.VMEM((rows * toks, width), F32),
            part(rows * toks, width),
            part(2, 2, classes // 2, toks),
            part(SIDE, SIDE, 2, 2, classes // 2, toks),
            part(classes, rows * toks),
            pltpu.SemaphoreType.DMA((copies,)),
            pltpu.SemaphoreType.DMA((copies,)),
        ],
        compiler_params=pltpu.CompilerParams(
            collective_id=1, has_side_effects=True, vmem_limit_bytes=60 * 1024 * 1024
        ),
    )(w, features, head, labels.reshape(1, toks))
    return loss.reshape(toks), wgrad, hgrad


def body(raw_weight, features, head, labels):
    current = raw_weight
    for _ in range(ITERS):
        current = bjorck_step(current)
    row_loss, weight_grad, head_grad = tail(current, features, head, labels)
    return (current, row_loss, weight_grad, head_grad)


def solution(mesh):
    placed = (P("row", "col"), P(None, "row"), P(None, "col"), P("row"))
    return jax.shard_map(
        body,
        mesh=mesh,
        in_specs=placed,
        out_specs=(P("row", "col"), P("row"), P("row", "col"), P(None, "col")),
        check_vma=False,
    )
```

```python
import jax
import jax.numpy as jnp
from jax import lax
from jax.experimental import pallas as pl
from jax.experimental.pallas import tpu as pltpu
from jax.sharding import PartitionSpec as P

CLASSES = 100
ITERS = 2
SIDE = 4
F32 = jnp.float32
BF16 = jnp.bfloat16
MESH = pl.DeviceIdType.MESH
NT = (((1,), (1,)), ((), ()))
TN = (((0,), (0,)), ((), ()))


class Copies:
    def __init__(self, send_sems, recv_sems):
        self.sems = (send_sems, recv_sems)
        self.count = 0
        self.started = {}
        self.leaving = {}

    def send(self, name, src, dst, device):
        copy = pltpu.make_async_remote_copy(
            src_ref=src, dst_ref=dst, send_sem=self.sems[0].at[self.count], recv_sem=self.sems[1].at[self.count],
            device_id=device, device_id_type=MESH,
        )
        self.count += 1
        copy.start()
        self.started[name] = self.leaving[name] = copy

    def arrived(self, name):
        self.started[name].wait_recv()

    def left(self, name):
        self.leaving.pop(name).wait_send()

    def drain(self):
        for name in list(self.leaving):
            self.left(name)
        self.started = {}


def neighbours():
    row, col = lax.axis_index("row"), lax.axis_index("col")
    x, z, y, core = row // SIDE, row % SIDE, col // 2, col % 2
    up = lambda v, d: (v + d) % SIDE
    return dict(
        zp=(x * SIDE + up(z, 1), col), zm=(x * SIDE + up(z, 3), col),
        xp=(up(x, 1) * SIDE + z, col), xm=(up(x, 3) * SIDE + z, col),
        yp=(row, up(y, 1) * 2 + core), ym=(row, up(y, 3) * 2 + core),
        twin=(row, y * 2 + 1 - core),
    )


def greet(devices):
    barrier = pltpu.get_barrier_semaphore()
    for device in devices:
        pl.semaphore_signal(barrier, inc=1, device_id=device, device_id_type=MESH)
    pl.semaphore_wait(barrier, len(devices))


def add_to(ref, *terms):
    total = ref[...].astype(F32)
    for term in terms:
        total = total + term[...].astype(F32)
    ref[...] = total.astype(ref.dtype)


PAIRS = (((1, 1), (0, 1)), ((1, 0), (0, 0)), ((1, 2), (2, 1)), ((2, 2), (1, 3)), ((2, 0), (0, 2)))
WHERE = {offset: (pair, which) for pair, both in enumerate(PAIRS) for which, offset in enumerate(both)}


def bjorck_step(net, to, w_ref, out_ref, local, remote):
    gp, gh, px1, px2, px3, pz1, pz2 = local
    az, ax, gr, gf, far, near, pfx, pqx, pfz, pqz, zr1, zr2 = remote
    rows, cols = w_ref.shape
    half, quarter, eighth, third = rows // 2, rows // 4, rows // 8, rows // 3
    col = lax.axis_index("col")
    y, core = col // 2, col % 2

    def block(dy, part=None):
        start = ((y + dy) % SIDE) * quarter
        if part is None:
            return pl.ds(pl.multiple_of(start, quarter), quarter)
        return pl.ds(pl.multiple_of(start + part * eighth, eighth), eighth)

    lo, hi = pl.ds(0, half), pl.ds(half, half)
    top, rest = pl.ds(0, third), pl.ds(third, rows - third)
    az[0] = w_ref[...].astype(BF16)
    own = az.at[0]
    net.send("zm0", own.at[top], az.at[1, top], to["zm"])
    net.send("xm0", own.at[lo], ax.at[1, lo], to["xm"])
    net.send("zp0", own.at[rest], az.at[3, rest], to["zp"])
    net.send("xp0", own.at[hi], ax.at[3, hi], to["xp"])
    net.send("zm1", own.at[rest], az.at[1, rest], to["zm"])
    net.send("xm1", own.at[hi], ax.at[1, hi], to["xm"])
    net.send("xp1", own.at[lo], ax.at[3, lo], to["xp"])
    ax[0] = az[0]
    net.arrived("zm0")
    net.send("zm2", az.at[1, top], az.at[2, top], to["zm"])
    net.arrived("xm0")
    net.send("xm2", ax.at[1, lo], ax.at[2, lo], to["xm"])
    net.arrived("xp0")
    net.send("xp2", ax.at[3, hi], ax.at[2, hi], to["xp"])
    net.arrived("zp0")
    net.send("zp2", az.at[3, rest], az.at[2, rest], to["zp"])
    needs = {0: ("zm1", "xm1"), 1: (), 2: ("xm2", "xp2", "zm2", "zp2"), 3: ("xp1",), 4: ()}

    def partial_gram(p):
        for name in needs[p]:
            net.arrived(name)
        for which, (dz, dx) in enumerate(PAIRS[p]):
            gp[p, which] = lax.dot_general(az[dz], ax[dx], NT, preferred_element_type=F32).astype(BF16)
        net.send(("twin", p), gp.at[p, 1 - core], gr.at[p], to["twin"])

    def chip_sum(p):
        net.arrived(("twin", p))
        gh[p] = (gp[p, core].astype(F32) + gr[p].astype(F32)).astype(BF16)
        net.send(("farp", p), gh.at[p, block(2, 0)], far.at[p, 0], to["yp"])
        net.send(("farm", p), gh.at[p, block(2, 1)], far.at[p, 1], to["ym"])

    def far_sum(p):
        net.arrived(("farp", p))
        add_to(gh.at[p, block(1, 0)], far.at[p, 0])
        net.send(("nearp", p), gh.at[p, block(1)], near.at[p, 0], to["yp"])
        net.arrived(("farm", p))
        add_to(gh.at[p, block(3, 1)], far.at[p, 1])
        net.send(("nearm", p), gh.at[p, block(3)], near.at[p, 1], to["ym"])

    def own_sum(p):
        net.arrived(("nearp", p))
        net.arrived(("nearm", p))
        piece = gf.at[p, core, block(0)]
        piece[...] = (gh[p, block(0)].astype(F32) + near[p, 0].astype(F32) + near[p, 1].astype(F32)).astype(BF16)
        for name in ("yp", "ym", "twin"):
            net.send(("own" + name, p), piece, piece, to[name])

    def pass_on(p):
        net.arrived(("ownym", p))
        piece = gf.at[p, core, block(1, 0)]
        net.send(("passm", p), piece, piece, to["ym"])
        net.arrived(("ownyp", p))
        piece = gf.at[p, core, block(3, 1)]
        net.send(("passp", p), piece, piece, to["yp"])
        for dy in (1, 3):
            piece = gf.at[p, core, block(dy)]
            net.send(("twin%d" % dy, p), piece, piece, to["twin"])

    def pass_far(p):
        net.arrived(("passm", p))
        net.arrived(("passp", p))
        piece = gf.at[p, core, block(2)]
        net.send(("twin2", p), piece, piece, to["twin"])

    def ready(p):
        for name in ("owntwin", "twin1", "twin3", "twin2"):
            net.arrived((name, p))

    def combine(direct, mirrored, put):
        @pl.loop(0, cols // 256)
        def _(n):
            at = pl.ds(pl.multiple_of(n * 256, 256), 256)
            acc = None
            for dz, dx in direct:
                term = jnp.dot(gf[WHERE[dz, dx]], ax[dx, :, at], preferred_element_type=F32)
                acc = term if acc is None else acc + term
            for dz, dx in mirrored:
                term = lax.dot_general(gf[WHERE[dz, dx]], az[dz, :, at], TN, preferred_element_type=F32)
                acc = term if acc is None else acc + term
            put(at, acc)

    def store(ref):
        def put(at, acc):
            ref[:, at] = acc.astype(BF16)
        return put

    def after_two():
        ready(0)
        ready(2)
        combine([], [(1, 2)], store(px2))
        net.send("x2p", px2.at[lo], pfx.at[0], to["xp"])
        net.send("x2m", px2.at[hi], pfx.at[1], to["xm"])
        combine([], [(1, 1), (2, 1), (0, 1)], store(px1))
        net.send("x1h", px1.at[hi], pqx.at[0, hi], to["xp"])

    def after_three():
        ready(1)
        ready(3)
        combine([(2, 1), (2, 2)], [], store(pz2))
        net.send("z2m", pz2.at[rest], zr1, to["zm"])
        net.send("z2p", pz2.at[top], pfz, to["zp"])
        combine([], [(1, 3)], store(px3))
        net.send("x3l", px3.at[lo], pqx.at[1, lo], to["xm"])
        combine([(1, 0), (1, 1), (1, 2), (1, 3)], [], store(pz1))
        net.send("z1r", pz1.at[rest], pqz.at[rest], to["zp"])
        net.arrived("x2p")
        add_to(px1.at[lo], pfx.at[0])
        net.send("x1l", px1.at[lo], pqx.at[0, lo], to["xp"])
        net.arrived("x2m")
        add_to(px3.at[hi], pfx.at[1])
        net.send("x3h", px3.at[hi], pqx.at[1, hi], to["xm"])

    def pass_sums():
        net.arrived("z2m")
        net.send("z2r", zr1, zr2, to["zm"])
        net.arrived("z2p")
        add_to(pz1.at[top], pfz)
        net.send("z1t", pz1.at[top], pqz.at[top], to["zp"])

    def after_four():
        ready(4)

        def put(at, acc):
            out_ref[:, at] = 1.5 * w_ref[:, at] - 0.5 * acc

        combine([(0, 0), (0, 1), (0, 2)], [(1, 0), (2, 0)], put)
        for name in ("x1h", "x3l", "z1r", "x1l", "x3h", "z2r", "z1t"):
            net.arrived(name)
        out_ref[top] -= 0.5 * (pqx[0, top].astype(F32) + pqx[1, top].astype(F32) + pqz[top].astype(F32))
        out_ref[rest] -= 0.5 * (
            pqx[0, rest].astype(F32) + pqx[1, rest].astype(F32) + pqz[rest].astype(F32) + zr2[...].astype(F32)
        )

    def run(*steps):
        for stage, p in steps:
            (partial_gram, chip_sum, far_sum, own_sum, pass_on, pass_far)[stage](p)

    run((0, 0), (0, 1), (1, 0), (1, 1), (2, 0), (2, 1))
    run((0, 2), (3, 0), (0, 3), (3, 1), (1, 2), (1, 3))
    run((4, 0), (2, 2), (4, 1), (2, 3), (0, 4))
    run((5, 0), (3, 2), (5, 1), (1, 4), (3, 3))
    run((4, 2), (2, 4), (4, 3))
    run((5, 2), (3, 4), (5, 3))
    after_two()
    run((4, 4))
    after_three()
    run((5, 4))
    pass_sums()
    after_four()


def bjorck_buffers(rows, cols):
    part = lambda *shape: pltpu.VMEM(shape, BF16)
    pairs, rest = len(PAIRS), rows - rows // 3
    local = [part(pairs, 2, rows, rows), part(pairs, rows, rows)] + [part(rows, cols)] * 5
    remote = [
        part(SIDE, rows, cols),
        part(SIDE, rows, cols),
        part(pairs, rows, rows),
        part(pairs, 2, rows, rows),
        part(pairs, 2, rows // 8, rows),
        part(pairs, 2, rows // 4, rows),
        part(2, rows // 2, cols),
        part(2, rows, cols),
        part(rows // 3, cols),
        part(rows, cols),
        part(rest, cols),
        part(rest, cols),
    ]
    return local, remote


def gather_ring(net, name, piece, first, second, plus, minus):
    net.send((name, "p"), piece(0), piece(0), plus)
    net.send((name, "m"), piece(0), piece(0), minus)

    def forward():
        net.arrived((name, "m"))
        net.send((name, "fm"), first(1), first(1), minus)
        net.arrived((name, "p"))
        net.send((name, "fp"), second(3), second(3), plus)

    def wait():
        net.arrived((name, "fm"))
        net.arrived((name, "fp"))

    return forward, wait


def whole_kernel(
    w_ref, feat_ref, given_head_ref, labels_ref, ortho_ref, loss_ref, wgrad_ref, hgrad_ref,
    local, first_remote, second_remote, head_ref, wb, pt, fa, na, fb, nb, sa, sb, f2a, n2a, f2b, n2b, kslots, lself, ltwin, lslots, act, active, slope, lfull, lgq, grads,
    send_sems, recv_sems,
):
    row, col = lax.axis_index("row"), lax.axis_index("col")
    x, z, y, core = row // SIDE, row % SIDE, col // 2, col % 2
    toks = labels_ref.shape[1]
    width = w_ref.shape[1]
    hcols = width // 2
    tok2 = toks // 2
    at = lambda v, d: (v + d) % SIDE
    to = neighbours()
    peers = [(row, at(y, dy) * 2 + (core + dk) % 2) for dy in range(SIDE) for dk in range(2) if (dy, dk) != (0, 0)]
    steps = sorted(((dx, dz) for dx in range(SIDE) for dz in range(SIDE) if (dx, dz) != (0, 0)), key=lambda d: -(d[0] == 2) - (d[1] == 2))
    plane = [(at(x, dx) * SIDE + at(z, dz), col) for dx, dz in steps]
    greet(plane + peers)
    net = Copies(send_sems, recv_sems)
    ca, cb = pl.ds(0, hcols), pl.ds(hcols, hcols)
    lo, hi = pl.ds(0, tok2), pl.ds(tok2, tok2)
    classes = head_ref.shape[0]
    real_classes = given_head_ref.shape[0]
    head_ref[...] = jnp.zeros_like(head_ref)
    head_ref[0:real_classes, :] = given_head_ref[...]
    kslots[col] = lax.dot_general(head_ref[...], head_ref[...], NT, preferred_element_type=F32)
    for peer, device in enumerate(peers):
        net.send(("k", peer), kslots.at[col], kslots.at[col], device)
    bjorck_step(net, to, w_ref, ortho_ref, local, first_remote)
    for peer in range(len(peers)):
        net.arrived(("k", peer))
    net.drain()
    bjorck_step(net, to, ortho_ref, ortho_ref, local, second_remote)
    net.drain()
    wb[...] = ortho_ref[...].astype(BF16)

    def forward(dx):
        start = pl.multiple_of(at(x, dx) * SIDE * toks, SIDE * toks)
        part = jnp.dot(feat_ref[pl.ds(start, SIDE * toks), :], wb[...], preferred_element_type=F32)
        pt[dx] = part.astype(BF16).reshape(SIDE, toks, width)

    forward(2)
    net.send("fap", pt.at[2, 0:2, :, ca], fa.at[0], to["xp"])
    net.send("fam", pt.at[2, 2:4, :, ca], fa.at[1], to["xm"])
    forward(1)
    net.send("nap1", pt.at[1, 2:4, :, ca], na.at[0, 2:4], to["xp"])
    forward(3)
    net.send("nam1", pt.at[3, 0:2, :, ca], na.at[1, 0:2], to["xm"])
    forward(0)
    net.send("fbp", pt.at[0:2, at(z, 2), :, cb], fb.at[0], to["zp"])
    net.send("fbm", pt.at[2:4, at(z, 2), :, cb], fb.at[1], to["zm"])
    net.send("nbp1", pt.at[2:4, at(z, 1), :, cb], nb.at[0, 2:4], to["zp"])
    net.send("nbm1", pt.at[0:2, at(z, 3), :, cb], nb.at[1, 0:2], to["zm"])
    net.arrived("fap")
    add_to(pt.at[1, 0:2, :, ca], fa.at[0])
    net.send("nap2", pt.at[1, 0:2, :, ca], na.at[0, 0:2], to["xp"])
    net.arrived("fam")
    add_to(pt.at[3, 2:4, :, ca], fa.at[1])
    net.send("nam2", pt.at[3, 2:4, :, ca], na.at[1, 2:4], to["xm"])

    net.arrived("fbp")
    add_to(pt.at[0:2, at(z, 1), :, cb], fb.at[0])
    net.send("nbp2", pt.at[0:2, at(z, 1), :, cb], nb.at[0, 0:2], to["zp"])
    net.arrived("fbm")
    add_to(pt.at[2:4, at(z, 3), :, cb], fb.at[1])
    net.send("nbm2", pt.at[2:4, at(z, 3), :, cb], nb.at[1, 2:4], to["zm"])

    def sum_a(dz):
        zz = at(z, dz)
        return pt[0, zz, :, ca].astype(F32) + na[0, zz].astype(F32) + na[1, zz].astype(F32)

    def sum_b(dx):
        return pt[dx, z, :, cb].astype(F32) + nb[0, dx].astype(F32) + nb[1, dx].astype(F32)

    for name in ("nap1", "nam1", "nap2", "nam2"):
        net.arrived(name)
    sa[2] = sum_a(2).astype(BF16)
    net.send("f2ap", sa.at[2, lo], f2a.at[0], to["zp"])
    net.send("f2am", sa.at[2, hi], f2a.at[1], to["zm"])
    sa[1] = sum_a(1).astype(BF16)
    net.send("n2ap1", sa.at[1, hi], n2a.at[0, hi], to["zp"])
    sa[3] = sum_a(3).astype(BF16)
    net.send("n2am1", sa.at[3, lo], n2a.at[1, lo], to["zm"])
    for name in ("nbp1", "nbm1", "nbp2", "nbm2"):
        net.arrived(name)
    sb[2] = sum_b(2).astype(BF16)
    net.send("f2bp", sb.at[2, lo], f2b.at[0], to["xp"])
    net.send("f2bm", sb.at[2, hi], f2b.at[1], to["xm"])
    sb[1] = sum_b(1).astype(BF16)
    net.send("n2bp1", sb.at[1, hi], n2b.at[0, hi], to["xp"])
    sb[3] = sum_b(3).astype(BF16)
    net.send("n2bm1", sb.at[3, lo], n2b.at[1, lo], to["xm"])
    net.arrived("f2ap")
    add_to(sa.at[1, lo], f2a.at[0])
    net.send("n2ap2", sa.at[1, lo], n2a.at[0, lo], to["zp"])
    net.arrived("f2am")
    add_to(sa.at[3, hi], f2a.at[1])
    net.send("n2am2", sa.at[3, hi], n2a.at[1, hi], to["zm"])
    net.arrived("f2bp")
    add_to(sb.at[1, lo], f2b.at[0])
    net.send("n2bp2", sb.at[1, lo], n2b.at[0, lo], to["xp"])
    net.arrived("f2bm")
    add_to(sb.at[3, hi], f2b.at[1])
    net.send("n2bm2", sb.at[3, hi], n2b.at[1, hi], to["xm"])
    own_a, own_b = sum_a(0), sum_b(0)

    for name in ("n2ap1", "n2am1", "n2ap2", "n2am2"):
        net.arrived(name)
    act[x, z, :, ca] = (own_a + n2a[0].astype(F32) + n2a[1].astype(F32)).astype(BF16)
    ga_forward, ga_wait = gather_ring(
        net, "ga", lambda d: act.at[at(x, d), z, :, ca], lambda d: act.at[at(x, d), z, lo, ca],
        lambda d: act.at[at(x, d), z, hi, ca], to["xp"], to["xm"],
    )
    for name in ("n2bp1", "n2bm1", "n2bp2", "n2bm2"):
        net.arrived(name)
    act[x, z, :, cb] = (own_b + n2b[0].astype(F32) + n2b[1].astype(F32)).astype(BF16)
    gb_forward, gb_wait = gather_ring(
        net, "gb", lambda d: act.at[x, at(z, d), :, cb], lambda d: act.at[x, at(z, d), lo, cb],
        lambda d: act.at[x, at(z, d), hi, cb], to["zp"], to["zm"],
    )
    own_act = jnp.tanh(act[x, z].astype(F32)).astype(BF16)
    lself[...] = lax.dot_general(head_ref[...], own_act, NT, preferred_element_type=F32)
    net.send("ltwin", lself, ltwin, to["twin"])

    pair_products = kslots[0]
    for other in range(1, 2 * SIDE):
        pair_products = pair_products + kslots[other]
    ids = lax.broadcasted_iota(jnp.int32, (classes, classes), 0)
    eye = ids == lax.broadcasted_iota(jnp.int32, (classes, classes), 1)
    class_ids = lax.broadcasted_iota(jnp.int32, (classes, toks), 0)
    one_hot = (class_ids == labels_ref[...]).astype(F32)
    high = lax.Precision.HIGHEST
    norms = jnp.sum(jnp.where(eye, pair_products, 0.0), axis=1, keepdims=True)
    inner = jnp.dot(pair_products, one_hot, precision=high, preferred_element_type=F32)
    own_norm = jnp.sum(one_hot * norms, axis=0, keepdims=True)
    distance = own_norm + norms - 2.0 * inner + 1e-05
    lipschitz = jnp.sqrt(jnp.where(one_hot > 0, 1.0, distance))

    net.arrived("ltwin")
    lslots[y] = (lself[...] + ltwin[...]).astype(BF16)
    for dy in (1, 2, 3):
        net.send(("l", dy), lslots.at[y], lslots.at[y], (row, at(y, dy) * 2 + core))
    ga_forward()
    gb_forward()
    for dy in (1, 2, 3):
        net.arrived(("l", dy))
    logits = lslots[0].astype(F32)
    for other in range(1, SIDE):
        logits = logits + lslots[other].astype(F32)
    real = (class_ids < CLASSES).astype(F32)
    plain_exp = real * jnp.exp(logits)
    bound_exp = (real - one_hot) * jnp.exp(logits + lipschitz)
    partition = jnp.sum(plain_exp, axis=0, keepdims=True) + jnp.sum(bound_exp, axis=0, keepdims=True)
    loss_ref[...] = jnp.log(partition) - jnp.sum(one_hot * logits, axis=0, keepdims=True)
    logit_grad = (plain_exp + bound_exp) / partition - one_hot
    dist_grad = bound_exp / (partition * 2.0 * lipschitz)
    pairs = lax.dot_general(one_hot, dist_grad, NT, precision=high, preferred_element_type=F32)
    pairs = pairs + lax.dot_general(dist_grad, one_hot, NT, precision=high, preferred_element_type=F32)
    for which, term in enumerate((logit_grad, pairs)):
        lfull[0, which] = term[0 : classes // 2].astype(BF16)
        lfull[1, which] = term[classes // 2 :].astype(BF16)
    lgq[x, z, core] = lfull[core]
    for peer, device in enumerate(plane):
        net.send(("g", peer), lgq.at[x, z, core], lgq.at[x, z, core], device)

    ga_wait()
    g2a_forward, g2a_wait = gather_ring(
        net, "g2a", lambda d: act.at[:, at(z, d), :, ca], lambda d: act.at[0:2, at(z, d), :, ca],
        lambda d: act.at[2:4, at(z, d), :, ca], to["zp"], to["zm"],
    )
    gb_wait()
    g2b_forward, g2b_wait = gather_ring(
        net, "g2b", lambda d: act.at[at(x, d), :, :, cb], lambda d: act.at[at(x, d), 0:2, :, cb],
        lambda d: act.at[at(x, d), 2:4, :, cb], to["xp"], to["xm"],
    )

    def activate(bx, bz, cols):
        tokens = pl.ds(pl.multiple_of((bx * SIDE + bz) * toks, toks), toks)
        value = jnp.tanh(act[bx, bz, :, cols].astype(F32))
        active[tokens, cols] = value.astype(BF16)
        slope[tokens, cols] = 1.0 - value * value

    def activate_both(d):
        @pl.loop(0, SIDE)
        def _(i):
            activate(i, at(z, d), ca)
            activate(at(x, d), i, cb)

    activate_both(0)
    for peer in range(len(plane)):
        net.arrived(("g", peer))
    net.send("gtwin", lgq.at[:, :, core], lgq.at[:, :, core], to["twin"])
    g2a_forward()
    g2b_forward()
    activate_both(1)
    activate_both(3)
    net.arrived("gtwin")
    total = jnp.zeros((classes, classes), F32)
    for block in range(SIDE * SIDE):
        bx, bz = block // SIDE, block % SIDE
        grads[:, block * toks : (block + 1) * toks] = lgq[bx, bz, :, 0].reshape(classes, toks)
        total = total + lgq[bx, bz, :, 1].reshape(classes, classes).astype(F32)
    laplace = jnp.where(eye, jnp.sum(total, axis=1, keepdims=True), 0.0) - total
    spread = 2.0 * jnp.dot(laplace, head_ref[...].astype(F32), precision=high, preferred_element_type=F32)
    hgrad_ref[...] = spread[0:real_classes]
    g2a_wait()
    g2b_wait()
    activate_both(2)

    for name in ("fap", "fam", "fbp", "fbm", "nap1", "nam1", "nbp1", "nbm1", "nap2", "nam2", "nbp2", "nbm2"):
        net.left(name)

    @pl.loop(0, SIDE)
    def _(block):
        tokens = pl.ds(pl.multiple_of(block * SIDE * toks, SIDE * toks), SIDE * toks)
        act_grad = lax.dot_general(grads[:, tokens], head_ref[...], TN, preferred_element_type=F32)
        pt[block] = (act_grad * slope[tokens, :]).astype(BF16).reshape(SIDE, toks, width)

    @pl.loop(0, width // 256)
    def _(n):
        cols = pl.ds(pl.multiple_of(n * 256, 256), 256)
        pre = pt[:, :, :, cols].reshape(SIDE * SIDE * toks, 256)
        wgrad_ref[:, cols] = lax.dot_general(feat_ref[...], pre, TN, preferred_element_type=F32)
        hgrad_ref[:, cols] += jnp.dot(grads[...], active[:, cols], preferred_element_type=F32)[0:real_classes]

    net.drain()


def body(raw_weight, features, head, labels):
    toks, width = labels.shape[0], head.shape[1]
    hcols, tok2, rows = width // 2, toks // 2, SIDE * SIDE
    classes = 128
    vmem = pl.BlockSpec(memory_space=pltpu.VMEM)
    local, remote = bjorck_buffers(*raw_weight.shape)
    copies = ITERS * (11 + 13 * len(PAIRS) + 11) + 7 + 12 + 12 + 16 + 1 + 3 + 15 + 1
    part = lambda *shape: pltpu.VMEM(shape, BF16)
    scratch = [
        tuple(local),
        tuple(remote),
        tuple(remote),
        part(classes, width),
        part(*raw_weight.shape),
        part(SIDE, SIDE, toks, width),
        part(2, 2, toks, hcols),
        part(2, SIDE, toks, hcols),
        part(2, 2, toks, hcols),
        part(2, SIDE, toks, hcols),
        part(SIDE, toks, hcols),
        part(SIDE, toks, hcols),
        part(2, tok2, hcols),
        part(2, toks, hcols),
        part(2, tok2, hcols),
        part(2, toks, hcols),
        pltpu.VMEM((2 * SIDE, classes, classes), F32),
        pltpu.VMEM((classes, toks), F32),
        pltpu.VMEM((classes, toks), F32),
        part(SIDE, classes, toks),
        part(SIDE, SIDE, toks, width),
        part(rows * toks, width),
        pltpu.VMEM((rows * toks, width), F32),
        part(2, 2, classes // 2, toks),
        part(SIDE, SIDE, 2, 2, classes // 2, toks),
        part(classes, rows * toks),
        pltpu.SemaphoreType.DMA((copies,)),
        pltpu.SemaphoreType.DMA((copies,)),
    ]
    ortho, loss, wgrad, hgrad = pl.pallas_call(
        whole_kernel,
        name="whole",
        out_shape=(
            jax.ShapeDtypeStruct(raw_weight.shape, F32),
            jax.ShapeDtypeStruct((1, toks), F32),
            jax.ShapeDtypeStruct(raw_weight.shape, F32),
            jax.ShapeDtypeStruct(head.shape, F32),
        ),
        in_specs=[vmem] * 4,
        out_specs=(vmem,) * 4,
        scratch_shapes=scratch,
        compiler_params=pltpu.CompilerParams(
            collective_id=0, has_side_effects=True, vmem_limit_bytes=67043328
        ),
    )(raw_weight, features, head, labels.reshape(1, toks))
    return ortho, loss.reshape(toks), wgrad, hgrad


def solution(mesh):
    placed = (P("row", "col"), P(None, "row"), P(None, "col"), P("row"))
    return jax.shard_map(
        body,
        mesh=mesh,
        in_specs=placed,
        out_specs=(P("row", "col"), P("row"), P("row", "col"), P(None, "col")),
        check_vma=False,
    )
```
